256 devices in a mesh: section: 64 (over z, x, core), atlas: 4 (over y).
Axes of the slice: x: 4, y: 4, z: 8, core: 2. Of those that a mesh axis runs over, the one named last changes fastest.
Arguments:
- counts: bfloat16 [131072, 5120], P(('section', 'atlas')), may hold values from -24 to 24
- gene_scale: float32 [5120], replicated, may hold values from 0.3 to 3
- cell_scale: float32 [131072], P(('section', 'atlas')), may hold values from 1 to 48
- gene_basis: bfloat16 [5120, 256], replicated, may hold values from -0.078125 to 0.078125
Outputs:
- cell_basis: bfloat16 [131072, 256], P(('section', 'atlas'))
- gene_side: float32 [5120, 256], P(('section', 'atlas'))
The draws below stay inside these ranges and needn't reach their ends.
All inputs are finite; a program needn't handle non-finite values.
Results may differ from the reference program's by a relative error of at most 0.0051.
Values sent between devices are 32-bit elements; how exact they have to be, the bound alone decides.
A program may use at most 64 MiB of HBM per device.

```python
import math
import jax
import jax.numpy as jnp
from jax import lax

GENES = 5120
RANK = 256
CELLS = 131072


def draw_cell_scale(key, part):
    ramp = jnp.exp(math.log(3.0) * jnp.arange(CELLS, dtype=jnp.float32) / (CELLS - 1))
    rough = jnp.exp(jax.random.uniform(key, (CELLS,), jnp.float32, 0.0, math.log(10.0)))
    return jnp.clip(ramp * rough, 1.0, 48.0).astype(jnp.float32)


def spiked(drawn, stream_key, source, target, shards_of, factor):
    def block_of(dim):
        return (jnp.arange(drawn.shape[dim]) // (drawn.shape[dim] // shards_of)).reshape((-1,) + (1,) * (drawn.ndim - 1 - dim))

    first = jax.random.permutation(stream_key, shards_of)[block_of(target)]
    far = (block_of(target) + shards_of // 2) % shards_of
    return jnp.where((block_of(source) == first) | (block_of(source) == far), factor * drawn, drawn)


def shard_levels(rng, dims, cuts, low, high):
    gain, own = 1.0, jax.random.fold_in(rng, 6)
    for position, shards_of in cuts:
        draws = jnp.exp(jax.random.uniform(jax.random.fold_in(own, position), (shards_of,), jnp.float32, low / len(cuts), high / len(cuts)))
        gain = gain * jnp.repeat(draws, dims[position] // shards_of).reshape([-1 if axis == position else 1 for axis in range(len(dims))])
    return gain


def centred(rng, extent, scale, reach, cuts=(), kind=jnp.bfloat16):
    values = jax.random.normal(rng, extent, jnp.float32) * scale
    if len(cuts) > 0:
        values = shard_levels(rng, extent, cuts, -0.22, 0.18) * values
    return jnp.clip(values, min=-reach, max=reach).astype(kind)


def bell_draw_with(own_key, extent, spread, bound, cuts, heavy, held_as=jnp.bfloat16):
    result = spread * jax.random.normal(own_key, extent, jnp.float32)
    if cuts:
        result = result * shard_levels(own_key, extent, cuts, -0.22, 0.18)
    return jnp.clip(spiked(result, jax.random.fold_in(own_key, 3), *heavy), -bound, bound).astype(held_as)


def setup_inputs(seed: int = 0) -> dict:
    arg_keys = jax.random.split(jax.random.key(seed), 5)
    return {
        "counts": bell_draw_with(arg_keys[0], (CELLS, GENES), 1.0, 24.0, ((0, 256),), (0, 1, 256, 6.0)),
        "gene_scale": jnp.clip(jnp.exp(jax.random.uniform(arg_keys[1], (GENES,), jnp.float32, math.log(0.3), math.log(3.0))), 0.3, 3.0),
        "cell_scale": draw_cell_scale(jax.random.fold_in(arg_keys[4], 71), 0),
        "gene_basis": centred(arg_keys[3], (GENES, RANK), GENES ** -0.5, 0.078125),
    }


def reference(counts, gene_scale, cell_scale, gene_basis):
    highest = lax.Precision.HIGHEST
    scaled = (gene_basis.astype(jnp.float32) * gene_scale[:, None]).astype(jnp.bfloat16)
    sketch = jnp.dot(counts.astype(jnp.float32), scaled.astype(jnp.float32), preferred_element_type=jnp.float32) * cell_scale[:, None]
    gram = jnp.dot(sketch.T.astype(jnp.float32), sketch.astype(jnp.float32), precision=highest, preferred_element_type=jnp.float32) / CELLS
    lower_factor = jnp.linalg.cholesky(gram)
    identity_matrix = jnp.eye(RANK, dtype=jnp.float32)
    inverse = jax.scipy.linalg.solve_triangular(lower_factor, identity_matrix, lower=True)
    orthonormal = jnp.dot(sketch.astype(jnp.float32), inverse.T.astype(jnp.float32), precision=highest, preferred_element_type=jnp.float32)
    cell_basis = orthonormal.astype(jnp.bfloat16)
    weighted = (sketch * cell_scale[:, None]).astype(jnp.bfloat16)
    sums = lax.dot_general(counts.astype(jnp.float32), weighted.astype(jnp.float32), (((0,), (0,)), ((), ())), preferred_element_type=jnp.float32)
    rotated = jnp.dot(sums.astype(jnp.float32), inverse.T.astype(jnp.float32), precision=highest, preferred_element_type=jnp.float32)
    gene_side = rotated * (gene_scale / CELLS)[:, None]
    return (cell_basis, gene_side)
```

```python
import functools

import jax
import jax.numpy as jnp
from jax import lax
from jax.experimental import pallas as pl
from jax.experimental.pallas import tpu as pltpu
from jax.sharding import PartitionSpec as P

HI = lax.Precision.HIGHEST
F32 = jnp.float32

def _sub(x, j):
    return jnp.broadcast_to(x[j:j + 1, :], x.shape)

def sweep(C, sub):
    C = list(C)
    Wt = [jnp.zeros((8, 128), F32) for _ in range(8)]
    piv = jnp.ones((8, 128), F32)
    for j in range(0, 8, 2):
        a, b, c = _sub(C[j], j), _sub(C[j], j + 1), _sub(C[j + 1], j + 1)
        r = 1.0 / (a * c - b * b)
        i11, i12, i22 = c * r, -b * r, a * r
        ra = 1.0 / a
        e = b * ra
        piv = jnp.where(sub == j, a, jnp.where(sub == j + 1, c - b * e, piv))
        for k in range(j):
            low = C[k] - e * _sub(C[k], j)
            Wt[k] = jnp.where(sub == j, C[k], jnp.where(sub == j + 1, low, Wt[k]))
        Wt[j] = jnp.where(sub == j, 1.0, jnp.where(sub == j + 1, -e, Wt[j]))
        Wt[j + 1] = jnp.where(sub == j + 1, 1.0, Wt[j + 1])
        for k in range(8):
            if k not in (j, j + 1):
                q0, q1 = _sub(C[k], j), _sub(C[k], j + 1)
                s0 = i11 * q0 + i12 * q1
                s1 = i12 * q0 + i22 * q1
                new = C[k] - (C[j] * s0 + C[j + 1] * s1)
                C[k] = jnp.where(sub == j, s0, jnp.where(sub == j + 1, s1, new))
        x, y = C[j], C[j + 1]
        C[j] = jnp.where(sub == j, i11, jnp.where(sub == j + 1, i12, -(x * i11 + y * i12)))
        C[j + 1] = jnp.where(sub == j, i12, jnp.where(sub == j + 1, i22, -(x * i12 + y * i22)))
    rs = lax.rsqrt(piv)
    return C, [w * rs for w in Wt]

def tree(xs):
    xs = list(xs)
    while len(xs) > 1:
        xs = [xs[i] + xs[i + 1] if i + 1 < len(xs) else xs[i] for i in range(0, len(xs), 2)]
    return xs[0]

def invchol128(M):
    n = len(M)
    M = list(M)
    sub = lax.broadcasted_iota(jnp.int32, (8, 128), 0)
    lane = lax.broadcasted_iota(jnp.int32, (8, 128), 1)
    out = []
    for k in range(n):
        blk = (lane >= 8 * k) & (lane < 8 * k + 8)
        Cb = [[jnp.broadcast_to(M[i][:, 8 * k + u:8 * k + u + 1], (8, 128)) for u in range(8)] for i in range(k, n)]
        m = jnp.where(blk, jnp.where(lane == 8 * k + sub, 1.0, 0.0), M[k])
        mb = [_sub(m, u) for u in range(8)]
        P, W8 = sweep(Cb[0], sub)
        T = tree([P[u] * mb[u] for u in range(8)])
        Tb = [_sub(T, u) for u in range(8)]
        for i in range(k + 1, n):
            M[i] = jnp.where(blk, 0.0, M[i]) - tree([Cb[i - k][u] * Tb[u] for u in range(8)])
        row = tree([W8[u] * mb[u] for u in range(8)])
        out.append(jnp.where(lane < 8 * k + 8, row, 0.0))
    return out

def dot(a, b, dims=((1,), (0,))):
    return lax.dot_general(a, b, (dims, ((), ())), precision=HI, preferred_element_type=F32)

def invchol256(g, w, between):
    o = invchol128([g[8 * i:8 * i + 8, 0:128] for i in range(16)])
    for i in range(16):
        w[8 * i:8 * i + 8, 0:128] = o[i]
        w[8 * i:8 * i + 8, 128:256] = jnp.zeros((8, 128), F32)
    w11 = w[0:128, 0:128]
    l21 = dot(g[128:256, 0:128], w11, ((1,), (1,)))
    g[128:256, 128:256] = g[128:256, 128:256] - dot(l21, l21, ((1,), (1,)))
    g[128:256, 0:128] = dot(l21, w11)
    between()
    o = invchol128([g[128 + 8 * i:136 + 8 * i, 128:256] for i in range(16)])
    for i in range(16):
        w[128 + 8 * i:136 + 8 * i, 128:256] = o[i]
    w[128:256, 0:128] = -dot(w[128:256, 128:256], g[128:256, 0:128])


MESH = pl.DeviceIdType.MESH
NZ, NX, NY = 8, 4, 4
PLANE = NX * NY * 2
CHUNKS = 10


def _wait(view, sem):
    pltpu.make_async_copy(view, view, sem).wait()


def _column(rows):
    r = rows.shape[0]
    return jnp.concatenate([rows, jnp.zeros((128 - r, 128), F32)], axis=0).T


class Ring4:
    def __init__(self, block, i, ids, plus, minus, sems, out):
        self.block, self.plus, self.minus, self.sems, self.out = block, plus, minus, sems, out
        self.i, self.ids = i, ids
        self.up, self.down, self.far = lax.rem(i + 1, 4), lax.rem(i + 3, 4), lax.rem(i + 2, 4)

    def send(self, q, owner, forward, slot):
        buf = self.plus if forward else self.minus
        pltpu.make_async_remote_copy(
            src_ref=self.block(q, owner),
            dst_ref=buf.at[slot],
            send_sem=self.sems.at[6 if forward else 7],
            recv_sem=self.sems.at[slot if forward else 3 + slot],
            device_id=self.ids(self.up if forward else self.down),
            device_id_type=MESH,
        ).start()

    def start(self):
        self.send(0, self.far, True, 0)
        self.send(1, self.far, False, 0)
        self.send(1, self.up, True, 1)
        self.send(0, self.down, False, 1)

    def middle(self):
        _wait(self.plus.at[0], self.sems.at[0])
        ref = self.block(0, self.up)
        ref[...] = ref[...] + self.plus[0]
        self.send(0, self.up, True, 2)
        _wait(self.minus.at[0], self.sems.at[3])
        ref = self.block(1, self.down)
        ref[...] = ref[...] + self.minus[0]
        self.send(1, self.down, False, 2)

    def finish(self):
        for s in (1, 2):
            _wait(self.plus.at[s], self.sems.at[s])
            _wait(self.minus.at[s], self.sems.at[3 + s])
        self.out[0] = self.block(0, self.i)[...] + (self.plus[2] + self.minus[1])
        self.out[1] = self.block(1, self.i)[...] + (self.plus[1] + self.minus[2])

    def drain(self):
        _wait(self.plus, self.sems.at[6])
        _wait(self.minus, self.sems.at[7])


def kernel(cells_all, counts, basis, scale, cells, cell_basis, gene_side,
           cbuf, bbuf, sbc, sk, wt, gl, gr, gp, zr, gz, gfull, g2, w, stg, S, R,
           XP, XM, YP, YM, PX, PY, X2P, X2M, Y2P, Y2M, Q, zs, z3,
           load_sem, gsem, csem, rsem, zsem):
    sec = lax.axis_index("section")
    y = lax.axis_index("atlas")
    c = lax.rem(sec, 2)
    x = lax.rem(sec // 2, NX)
    z = sec // (2 * NX)
    p = (x * NY + y) * 2 + c

    def plane_id(q):
        return ((z * NX + q // (2 * NY)) * 2 + lax.rem(q, 2), lax.rem(q // 2, NY))

    def z_id(k):
        return ((k * NX + x) * 2 + c, y)

    def x_id(k):
        return ((z * NX + k) * 2 + c, y)

    def y_id(k):
        return (sec, k)

    partner = (sec + 1 - 2 * c, y)
    step = counts.shape[1] // CHUNKS

    def loads(k):
        cols = pl.ds(pl.multiple_of(k * step, step), step)
        return (pltpu.make_async_copy(counts.at[:, cols], cbuf.at[:, cols], load_sem.at[0, k]),
                pltpu.make_async_copy(basis.at[cols, :], bbuf.at[cols, :], load_sem.at[1, k]))

    for k in range(CHUNKS):
        for copy in loads(k):
            copy.start()

    barrier = pltpu.get_barrier_semaphore()

    @pl.loop(1, PLANE)
    def _(d):
        pl.semaphore_signal(barrier, inc=1, device_id=plane_id(lax.rem(p + d, PLANE)), device_id_type=MESH)

    @pl.loop(1, NZ)
    def _(d):
        pl.semaphore_signal(barrier, inc=1, device_id=z_id(lax.rem(z + d, NZ)), device_id_type=MESH)

    turned = _column(scale[...])
    for g in range(scale.shape[0]):
        sbc[128 * g:128 * g + 128, :] = jnp.broadcast_to(turned[:, g:g + 1], (128, 128))

    sk[...] = jnp.zeros_like(sk)

    @pl.loop(0, CHUNKS)
    def _(k):
        for copy in loads(k):
            copy.wait()
        rows = pl.ds(pl.multiple_of(k * step, step), step)
        factor = sbc[rows, :]
        part = bbuf[rows, :].astype(F32)
        scaled = jnp.concatenate([part[:, :128] * factor, part[:, 128:] * factor], axis=1).astype(jnp.bfloat16)
        sk[...] += jnp.dot(cbuf[:, rows], scaled, preferred_element_type=F32)

    turned = _column(cells[...])
    for r in range(cells.shape[0]):
        rows = slice(128 * r, 128 * r + 128)
        factor = jnp.broadcast_to(turned[:, r:r + 1], (128, 256))
        value = sk[rows, :] * factor
        sk[rows, :] = value
        wt[rows, :] = (value * factor).astype(jnp.bfloat16)

    gram = dot(sk[...], sk[...], ((0,), (0,))) * (1.0 / cells_all)
    gl[...] = gram.reshape(PLANE, 8, 256)

    pl.semaphore_wait(barrier, PLANE - 1 + NZ - 1)

    @pl.loop(1, PLANE)
    def _(d):
        q = lax.rem(p + d, PLANE)
        pltpu.make_async_remote_copy(
            src_ref=gl.at[q], dst_ref=gr.at[d - 1], send_sem=gsem.at[0], recv_sem=gsem.at[1],
            device_id=plane_id(q), device_id_type=MESH).start()

    @pl.loop(0, NZ)
    def _(k):
        cols = pl.ds(pl.multiple_of(k * 640, 640), 640)
        part = lax.dot_general(cbuf[:, cols], wt[...], (((0,), (0,)), ((), ())), preferred_element_type=F32)
        factor = sbc[cols, :] * (1.0 / cells_all)
        stg[:, :128] = part[:, :128] * factor
        stg[:, 128:] = part[:, 128:] * factor
        for a in range(NX):
            for b in range(2):
                for e in range(NY):
                    o = ((a * 2 + b) * NY + e) * 20
                    S[b, 0, k, a, e] = stg[o:o + 8, :128]
                    S[b, 1, k, a, e] = stg[o:o + 8, 128:]
                    S[b, 2, k, a, e] = stg[o + 8:o + 16, :128]
                    S[b, 3, k, a, e] = stg[o + 8:o + 16, 128:]
                    S[b, k // 2, 8 + lax.rem(k, 2), a, e] = jnp.concatenate(
                        [stg[o + 16:o + 20, :128], stg[o + 16:o + 20, 128:]], axis=0)
        pltpu.make_async_remote_copy(
            src_ref=S.at[1 - c, :, k], dst_ref=R.at[:, k], send_sem=csem.at[0], recv_sem=csem.at[1],
            device_id=partner, device_id_type=MESH).start()

    pltpu.make_async_remote_copy(
        src_ref=S.at[1 - c, :, 8:10], dst_ref=R.at[:, 8:10], send_sem=csem.at[0], recv_sem=csem.at[1],
        device_id=partner, device_id_type=MESH).start()

    _wait(gr, gsem.at[1])
    gp[...] = gl[p] + jnp.sum(gr[...], axis=0)

    @pl.loop(1, NZ)
    def _(d):
        pltpu.make_async_remote_copy(
            src_ref=gp, dst_ref=zr.at[d - 1], send_sem=gsem.at[2], recv_sem=gsem.at[3],
            device_id=z_id(lax.rem(z + d, NZ)), device_id_type=MESH).start()

    _wait(R, csem.at[1])

    @pl.loop(0, 10)
    def _(u):
        for q in range(4):
            R[q, u] = R[q, u] + S[c, q, u]

    first = Ring4(lambda q, o: R.at[q, :, o], x, x_id, XP, XM, rsem.at[0], PX)
    second = Ring4(lambda q, o: R.at[2 + q, :, :, o], y, y_id, YP, YM, rsem.at[1], PY)
    first.start()
    second.start()

    _wait(zr, gsem.at[3])
    gz[...] = gp[...] + jnp.sum(zr[...], axis=0)
    gfull[p] = gz[...]

    @pl.loop(1, PLANE)
    def _(d):
        pltpu.make_async_remote_copy(
            src_ref=gz, dst_ref=gfull.at[p], send_sem=gsem.at[4], recv_sem=gsem.at[5],
            device_id=plane_id(lax.rem(p + d, PLANE)), device_id_type=MESH).start()

    first.middle()
    second.middle()

    _wait(gfull.at[0:PLANE - 1], gsem.at[5])
    g2[...] = gfull[...].reshape(256, 256)

    third = Ring4(lambda q, o: PX.at[q, :, o], y, y_id, X2P, X2M, rsem.at[2], Q.at[0:2])
    fourth = Ring4(lambda q, o: PY.at[q, :, o], x, x_id, Y2P, Y2M, rsem.at[3], Q.at[2:4])

    def after_half():
        first.finish()
        second.finish()
        third.start()
        fourth.start()
        third.middle()
        fourth.middle()

    invchol256(g2, w, after_half)

    third.finish()
    fourth.finish()
    for k in range(NZ):
        for t in range(4):
            zs[k, t] = Q[t, k]
        zs[k, 4] = Q[k // 2, 8 + k % 2]

    @pl.loop(1, NZ)
    def _(d):
        k = lax.rem(z + d, NZ)
        pltpu.make_async_remote_copy(
            src_ref=zs.at[k], dst_ref=z3.at[d - 1], send_sem=zsem.at[0], recv_sem=zsem.at[1],
            device_id=z_id(k), device_id_type=MESH).start()

    cell_basis[...] = dot(sk[...], w[...], ((1,), (1,))).astype(jnp.bfloat16)

    _wait(z3, zsem.at[1])
    own = zs[z] + jnp.sum(z3[...], axis=0)
    top = jnp.concatenate([own[0], own[1]], axis=1)
    mid = jnp.concatenate([own[2], own[3]], axis=1)
    low = jnp.concatenate([own[4], pltpu.roll(own[4], 4, 0)], axis=1)
    side = dot(jnp.concatenate([top, mid, low], axis=0), w[...], ((1,), (1,)))
    gene_side[...] = side[:20]

    _wait(gr, gsem.at[0])
    _wait(zr, gsem.at[2])
    _wait(gfull.at[0:PLANE - 1], gsem.at[4])
    _wait(R, csem.at[0])
    for ring in (first, second, third, fourth):
        ring.drain()
    _wait(z3, zsem.at[0])


def local(counts, gene_scale, cell_scale, gene_basis):
    device_count = lax.axis_size("section") * lax.axis_size("atlas")
    rows, genes = counts.shape
    vm = lambda *s: pltpu.VMEM(s, F32)
    dma = pltpu.SemaphoreType.DMA
    return pl.pallas_call(
        functools.partial(kernel, rows * device_count),
        out_shape=(jax.ShapeDtypeStruct((rows, 256), jnp.bfloat16),
                   jax.ShapeDtypeStruct((genes // device_count, 256), F32)),
        in_specs=[pl.BlockSpec(memory_space=pl.ANY)] * 2 + [pl.BlockSpec(memory_space=pltpu.VMEM)] * 2,
        out_specs=(pl.BlockSpec(memory_space=pltpu.VMEM),) * 2,
        scratch_shapes=[
            pltpu.VMEM((rows, genes), jnp.bfloat16), pltpu.VMEM((genes, 256), jnp.bfloat16),
            vm(genes, 128), vm(rows, 256), pltpu.VMEM((rows, 256), jnp.bfloat16),
            vm(PLANE, 8, 256), vm(PLANE - 1, 8, 256), vm(8, 256), vm(NZ - 1, 8, 256), vm(8, 256),
            vm(PLANE, 8, 256), vm(256, 256), vm(256, 256), vm(640, 256),
            vm(2, 4, 10, NX, NY, 8, 128), vm(4, 10, NX, NY, 8, 128),
            vm(3, 10, 4, 8, 128), vm(3, 10, 4, 8, 128), vm(3, 10, 4, 8, 128), vm(3, 10, 4, 8, 128),
            vm(2, 10, 4, 8, 128), vm(2, 10, 4, 8, 128),
            vm(3, 10, 8, 128), vm(3, 10, 8, 128), vm(3, 10, 8, 128), vm(3, 10, 8, 128),
            vm(4, 10, 8, 128), vm(NZ, 5, 8, 128), vm(NZ - 1, 5, 8, 128),
            dma((2, CHUNKS)), dma((6,)), dma((2,)), dma((4, 8)), dma((2,)),
        ],
        compiler_params=pltpu.CompilerParams(collective_id=0, has_side_effects=True, vmem_limit_bytes=60 << 20),
    )(counts, gene_basis, gene_scale.reshape(genes // 128, 128), cell_scale.reshape(rows // 128, 128))


def solution(mesh):
    return jax.shard_map(
        local,
        mesh=mesh,
        in_specs=(P(("section", "atlas"), None), P(), P(("section", "atlas")), P()),
        out_specs=(P(("section", "atlas"), None), P(("section", "atlas"), None)),
        check_vma=False,
    )
```

```python
import functools

import jax
import jax.numpy as jnp
from jax import lax
from jax.experimental import pallas as pl
from jax.experimental.pallas import tpu as pltpu
from jax.sharding import PartitionSpec as P

HI = lax.Precision.HIGHEST
F32 = jnp.float32

def _sub(x, j):
    return jnp.broadcast_to(x[j:j + 1, :], x.shape)

def sweep(C, sub):
    C = list(C)
    Wt = [jnp.zeros((8, 128), F32) for _ in range(8)]
    piv = jnp.ones((8, 128), F32)
    for j in range(0, 8, 2):
        a, b, c = _sub(C[j], j), _sub(C[j], j + 1), _sub(C[j + 1], j + 1)
        r = 1.0 / (a * c - b * b)
        i11, i12, i22 = c * r, -b * r, a * r
        ra = 1.0 / a
        e = b * ra
        piv = jnp.where(sub == j, a, jnp.where(sub == j + 1, c - b * e, piv))
        for k in range(j):
            low = C[k] - e * _sub(C[k], j)
            Wt[k] = jnp.where(sub == j, C[k], jnp.where(sub == j + 1, low, Wt[k]))
        Wt[j] = jnp.where(sub == j, 1.0, jnp.where(sub == j + 1, -e, Wt[j]))
        Wt[j + 1] = jnp.where(sub == j + 1, 1.0, Wt[j + 1])
        for k in range(8):
            if k not in (j, j + 1):
                q0, q1 = _sub(C[k], j), _sub(C[k], j + 1)
                s0 = i11 * q0 + i12 * q1
                s1 = i12 * q0 + i22 * q1
                new = C[k] - (C[j] * s0 + C[j + 1] * s1)
                C[k] = jnp.where(sub == j, s0, jnp.where(sub == j + 1, s1, new))
        x, y = C[j], C[j + 1]
        C[j] = jnp.where(sub == j, i11, jnp.where(sub == j + 1, i12, -(x * i11 + y * i12)))
        C[j + 1] = jnp.where(sub == j, i12, jnp.where(sub == j + 1, i22, -(x * i12 + y * i22)))
    rs = lax.rsqrt(piv)
    return C, [w * rs for w in Wt]

def tree(xs):
    xs = list(xs)
    while len(xs) > 1:
        xs = [xs[i] + xs[i + 1] if i + 1 < len(xs) else xs[i] for i in range(0, len(xs), 2)]
    return xs[0]

def invchol128(M, hook):
    n = len(M)
    M = list(M)
    sub = lax.broadcasted_iota(jnp.int32, (8, 128), 0)
    lane = lax.broadcasted_iota(jnp.int32, (8, 128), 1)
    out = []
    for k in range(n):
        hook(k)
        blk = (lane >= 8 * k) & (lane < 8 * k + 8)
        Cb = [[jnp.broadcast_to(M[i][:, 8 * k + u:8 * k + u + 1], (8, 128)) for u in range(8)] for i in range(k, n)]
        m = jnp.where(blk, jnp.where(lane == 8 * k + sub, 1.0, 0.0), M[k])
        mb = [_sub(m, u) for u in range(8)]
        P, W8 = sweep(Cb[0], sub)
        T = tree([P[u] * mb[u] for u in range(8)])
        Tb = [_sub(T, u) for u in range(8)]
        for i in range(k + 1, n):
            M[i] = jnp.where(blk, 0.0, M[i]) - tree([Cb[i - k][u] * Tb[u] for u in range(8)])
        row = tree([W8[u] * mb[u] for u in range(8)])
        out.append(jnp.where(lane < 8 * k + 8, row, 0.0))
    return out

def dot(a, b, dims=((1,), (0,))):
    return lax.dot_general(a, b, (dims, ((), ())), precision=HI, preferred_element_type=F32)

def invchol256(g, w, hook):
    o = invchol128([g[8 * i:8 * i + 8, 0:128] for i in range(16)], lambda k: hook(0, k))
    for i in range(16):
        w[8 * i:8 * i + 8, 0:128] = o[i]
        w[8 * i:8 * i + 8, 128:256] = jnp.zeros((8, 128), F32)
    w11 = w[0:128, 0:128]
    l21 = dot(g[128:256, 0:128], w11, ((1,), (1,)))
    g[128:256, 128:256] = g[128:256, 128:256] - dot(l21, l21, ((1,), (1,)))
    g[128:256, 0:128] = dot(l21, w11)
    o = invchol128([g[128 + 8 * i:136 + 8 * i, 128:256] for i in range(16)], lambda k: hook(1, k))
    for i in range(16):
        w[128 + 8 * i:136 + 8 * i, 128:256] = o[i]
    w[128:256, 0:128] = -dot(w[128:256, 128:256], g[128:256, 0:128])


MESH = pl.DeviceIdType.MESH
NZ, NX, NY = 8, 4, 4
PLANE = NX * NY * 2
CHUNKS = 10


def _wait(view, sem):
    pltpu.make_async_copy(view, view, sem).wait()


def _column(rows):
    r = rows.shape[0]
    return jnp.concatenate([rows, jnp.zeros((128 - r, 128), F32)], axis=0).T


class Ring4:
    def __init__(self, block, i, ids, plus, minus, sems, out):
        self.block, self.plus, self.minus, self.sems, self.out = block, plus, minus, sems, out
        self.i, self.ids = i, ids
        self.up, self.down, self.far = lax.rem(i + 1, 4), lax.rem(i + 3, 4), lax.rem(i + 2, 4)

    def send(self, q, owner, forward, slot):
        buf = self.plus if forward else self.minus
        pltpu.make_async_remote_copy(
            src_ref=self.block(q, owner),
            dst_ref=buf.at[slot],
            send_sem=self.sems.at[6 if forward else 7],
            recv_sem=self.sems.at[slot if forward else 3 + slot],
            device_id=self.ids(self.up if forward else self.down),
            device_id_type=MESH,
        ).start()

    def start(self):
        self.send(0, self.far, True, 0)
        self.send(1, self.far, False, 0)
        self.send(1, self.up, True, 1)
        self.send(0, self.down, False, 1)

    def middle(self):
        _wait(self.plus.at[0], self.sems.at[0])
        ref = self.block(0, self.up)
        ref[...] = ref[...] + self.plus[0]
        self.send(0, self.up, True, 2)
        _wait(self.minus.at[0], self.sems.at[3])
        ref = self.block(1, self.down)
        ref[...] = ref[...] + self.minus[0]
        self.send(1, self.down, False, 2)

    def finish(self):
        for s in (1, 2):
            _wait(self.plus.at[s], self.sems.at[s])
            _wait(self.minus.at[s], self.sems.at[3 + s])
        self.out[0] = self.block(0, self.i)[...] + (self.plus[2] + self.minus[1])
        self.out[1] = self.block(1, self.i)[...] + (self.plus[1] + self.minus[2])

    def drain(self):
        _wait(self.plus, self.sems.at[6])
        _wait(self.minus, self.sems.at[7])


def kernel(cells_all, counts, basis, scale, cells, cell_basis, gene_side,
           cbuf, bbuf, sbc, sk, wt, gl, gr, gp, zr, gz, gfull, g2, w, stg, S, R,
           XP, XM, YP, YM, PX, PY, X2P, X2M, Y2P, Y2M, Q, zs, z3,
           load_sem, gsem, csem, rsem, zsem):
    sec = lax.axis_index("section")
    y = lax.axis_index("atlas")
    c = lax.rem(sec, 2)
    x = lax.rem(sec // 2, NX)
    z = sec // (2 * NX)
    p = (x * NY + y) * 2 + c

    def plane_id(q):
        return ((z * NX + q // (2 * NY)) * 2 + lax.rem(q, 2), lax.rem(q // 2, NY))

    def z_id(k):
        return ((k * NX + x) * 2 + c, y)

    def x_id(k):
        return ((z * NX + k) * 2 + c, y)

    def y_id(k):
        return (sec, k)

    partner = (sec + 1 - 2 * c, y)
    step = counts.shape[1] // CHUNKS

    def loads(k):
        cols = pl.ds(pl.multiple_of(k * step, step), step)
        return (pltpu.make_async_copy(counts.at[:, cols], cbuf.at[:, cols], load_sem.at[0, k]),
                pltpu.make_async_copy(basis.at[cols, :], bbuf.at[cols, :], load_sem.at[1, k]))

    for k in range(CHUNKS):
        for copy in loads(k):
            copy.start()

    barrier = pltpu.get_barrier_semaphore()

    @pl.loop(1, PLANE)
    def _(d):
        pl.semaphore_signal(barrier, inc=1, device_id=plane_id(lax.rem(p + d, PLANE)), device_id_type=MESH)

    @pl.loop(1, NZ)
    def _(d):
        pl.semaphore_signal(barrier, inc=1, device_id=z_id(lax.rem(z + d, NZ)), device_id_type=MESH)

    turned = _column(scale[...])
    for g in range(scale.shape[0]):
        sbc[128 * g:128 * g + 128, :] = jnp.broadcast_to(turned[:, g:g + 1], (128, 128))

    sk[...] = jnp.zeros_like(sk)

    @pl.loop(0, CHUNKS)
    def _(k):
        for copy in loads(k):
            copy.wait()
        rows = pl.ds(pl.multiple_of(k * step, step), step)
        factor = sbc[rows, :]
        part = bbuf[rows, :].astype(F32)
        scaled = jnp.concatenate([part[:, :128] * factor, part[:, 128:] * factor], axis=1).astype(jnp.bfloat16)
        sk[...] += jnp.dot(cbuf[:, rows], scaled, preferred_element_type=F32)

    turned = _column(cells[...])
    for r in range(cells.shape[0]):
        rows = slice(128 * r, 128 * r + 128)
        factor = jnp.broadcast_to(turned[:, r:r + 1], (128, 256))
        value = sk[rows, :] * factor
        sk[rows, :] = value
        wt[rows, :] = (value * factor).astype(jnp.bfloat16)

    gram = dot(sk[...], sk[...], ((0,), (0,))) * (1.0 / cells_all)
    gl[...] = gram.reshape(PLANE, 8, 256)

    pl.semaphore_wait(barrier, PLANE - 1 + NZ - 1)

    @pl.loop(1, PLANE)
    def _(d):
        q = lax.rem(p + d, PLANE)
        pltpu.make_async_remote_copy(
            src_ref=gl.at[q], dst_ref=gr.at[d - 1], send_sem=gsem.at[0], recv_sem=gsem.at[1],
            device_id=plane_id(q), device_id_type=MESH).start()

    @pl.loop(0, NZ)
    def _(k):
        cols = pl.ds(pl.multiple_of(k * 640, 640), 640)
        part = lax.dot_general(cbuf[:, cols], wt[...], (((0,), (0,)), ((), ())), preferred_element_type=F32)
        factor = sbc[cols, :] * (1.0 / cells_all)
        stg[:, :128] = part[:, :128] * factor
        stg[:, 128:] = part[:, 128:] * factor
        for a in range(NX):
            for b in range(2):
                for e in range(NY):
                    o = ((a * 2 + b) * NY + e) * 20
                    S[b, 0, k, a, e] = stg[o:o + 8, :128]
                    S[b, 1, k, a, e] = stg[o:o + 8, 128:]
                    S[b, 2, k, a, e] = stg[o + 8:o + 16, :128]
                    S[b, 3, k, a, e] = stg[o + 8:o + 16, 128:]
                    S[b, k // 2, 8 + lax.rem(k, 2), a, e] = jnp.concatenate(
                        [stg[o + 16:o + 20, :128], stg[o + 16:o + 20, 128:]], axis=0)
        pltpu.make_async_remote_copy(
            src_ref=S.at[1 - c, :, k], dst_ref=R.at[:, k], send_sem=csem.at[0], recv_sem=csem.at[1],
            device_id=partner, device_id_type=MESH).start()

    pltpu.make_async_remote_copy(
        src_ref=S.at[1 - c, :, 8:10], dst_ref=R.at[:, 8:10], send_sem=csem.at[0], recv_sem=csem.at[1],
        device_id=partner, device_id_type=MESH).start()

    _wait(gr, gsem.at[1])
    gp[...] = gl[p] + jnp.sum(gr[...], axis=0)

    @pl.loop(1, NZ)
    def _(d):
        pltpu.make_async_remote_copy(
            src_ref=gp, dst_ref=zr.at[d - 1], send_sem=gsem.at[2], recv_sem=gsem.at[3],
            device_id=z_id(lax.rem(z + d, NZ)), device_id_type=MESH).start()

    _wait(R, csem.at[1])

    @pl.loop(0, 10)
    def _(u):
        for q in range(4):
            R[q, u] = R[q, u] + S[c, q, u]

    first = Ring4(lambda q, o: R.at[q, :, o], x, x_id, XP, XM, rsem.at[0], PX)
    second = Ring4(lambda q, o: R.at[2 + q, :, :, o], y, y_id, YP, YM, rsem.at[1], PY)
    first.start()
    second.start()

    first.middle()
    second.middle()

    _wait(zr, gsem.at[3])
    gz[...] = gp[...] + jnp.sum(zr[...], axis=0)
    gfull[p] = gz[...]

    @pl.loop(1, PLANE)
    def _(d):
        pltpu.make_async_remote_copy(
            src_ref=gz, dst_ref=gfull.at[p], send_sem=gsem.at[4], recv_sem=gsem.at[5],
            device_id=plane_id(lax.rem(p + d, PLANE)), device_id_type=MESH).start()

    _wait(gfull.at[0:PLANE - 1], gsem.at[5])
    g2[...] = gfull[...].reshape(256, 256)

    third = Ring4(lambda q, o: PX.at[q, :, o], y, y_id, X2P, X2M, rsem.at[2], Q.at[0:2])
    fourth = Ring4(lambda q, o: PY.at[q, :, o], x, x_id, Y2P, Y2M, rsem.at[3], Q.at[2:4])

    def hook(half, k):
        if (half, k) == (0, 0):
            first.finish()
            second.finish()
            third.start()
            fourth.start()
        elif (half, k) == (0, 8):
            third.middle()
            fourth.middle()
        elif (half, k) == (1, 0):
            third.finish()
            fourth.finish()
            for i in range(NZ):
                for t in range(4):
                    zs[i, t] = Q[t, i]
                zs[i, 4] = Q[i // 2, 8 + i % 2]

            @pl.loop(1, NZ)
            def _(d):
                i = lax.rem(z + d, NZ)
                pltpu.make_async_remote_copy(
                    src_ref=zs.at[i], dst_ref=z3.at[d - 1], send_sem=zsem.at[0], recv_sem=zsem.at[1],
                    device_id=z_id(i), device_id_type=MESH).start()

    invchol256(g2, w, hook)

    cell_basis[...] = dot(sk[...], w[...], ((1,), (1,))).astype(jnp.bfloat16)

    _wait(z3, zsem.at[1])
    own = zs[z] + jnp.sum(z3[...], axis=0)
    top = jnp.concatenate([own[0], own[1]], axis=1)
    mid = jnp.concatenate([own[2], own[3]], axis=1)
    low = jnp.concatenate([own[4], pltpu.roll(own[4], 4, 0)], axis=1)
    side = dot(jnp.concatenate([top, mid, low], axis=0), w[...], ((1,), (1,)))
    gene_side[...] = side[:20]

    _wait(gr, gsem.at[0])
    _wait(zr, gsem.at[2])
    _wait(gfull.at[0:PLANE - 1], gsem.at[4])
    _wait(R, csem.at[0])
    for ring in (first, second, third, fourth):
        ring.drain()
    _wait(z3, zsem.at[0])


def hand_on(a, b, a_out, b_out):
    a_out[...] = a[...]
    b_out[...] = b[...]


def local(counts, gene_scale, cell_scale, gene_basis):
    device_count = lax.axis_size("section") * lax.axis_size("atlas")
    rows, genes = counts.shape
    vm = lambda *s: pltpu.VMEM(s, F32)
    dma = pltpu.SemaphoreType.DMA
    shapes = (jax.ShapeDtypeStruct((rows, 256), jnp.bfloat16),
              jax.ShapeDtypeStruct((genes // device_count, 256), F32))
    result = pl.pallas_call(
        functools.partial(kernel, rows * device_count),
        out_shape=shapes,
        in_specs=[pl.BlockSpec(memory_space=pl.ANY)] * 2 + [pl.BlockSpec(memory_space=pltpu.VMEM)] * 2,
        out_specs=(pl.BlockSpec(memory_space=pltpu.VMEM),) * 2,
        scratch_shapes=[
            pltpu.VMEM((rows, genes), jnp.bfloat16), pltpu.VMEM((genes, 256), jnp.bfloat16),
            vm(genes, 128), vm(rows, 256), pltpu.VMEM((rows, 256), jnp.bfloat16),
            vm(PLANE, 8, 256), vm(PLANE - 1, 8, 256), vm(8, 256), vm(NZ - 1, 8, 256), vm(8, 256),
            vm(PLANE, 8, 256), vm(256, 256), vm(256, 256), vm(640, 256),
            vm(2, 4, 10, NX, NY, 8, 128), vm(4, 10, NX, NY, 8, 128),
            vm(3, 10, 4, 8, 128), vm(3, 10, 4, 8, 128), vm(3, 10, 4, 8, 128), vm(3, 10, 4, 8, 128),
            vm(2, 10, 4, 8, 128), vm(2, 10, 4, 8, 128),
            vm(3, 10, 8, 128), vm(3, 10, 8, 128), vm(3, 10, 8, 128), vm(3, 10, 8, 128),
            vm(4, 10, 8, 128), vm(NZ, 5, 8, 128), vm(NZ - 1, 5, 8, 128),
            dma((2, CHUNKS)), dma((6,)), dma((2,)), dma((4, 8)), dma((2,)),
        ],
        compiler_params=pltpu.CompilerParams(collective_id=0, has_side_effects=True, vmem_limit_bytes=60 << 20),
    )(counts, gene_basis, gene_scale.reshape(genes // 128, 128), cell_scale.reshape(rows // 128, 128))
    return pl.pallas_call(hand_on, out_shape=shapes)(*result)


def solution(mesh):
    return jax.shard_map(
        local,
        mesh=mesh,
        in_specs=(P(("section", "atlas"), None), P(), P(("section", "atlas")), P()),
        out_specs=(P(("section", "atlas"), None), P(("section", "atlas"), None)),
        check_vma=False,
    )
```

```python
import functools

import jax
import jax.numpy as jnp
from jax import lax
from jax.experimental import pallas as pl
from jax.experimental.pallas import tpu as pltpu
from jax.sharding import PartitionSpec as P

HI = lax.Precision.HIGHEST
F32 = jnp.float32

def _sub(x, j):
    return jnp.broadcast_to(x[j:j + 1, :], x.shape)

def sweep(C, sub):
    C = list(C)
    Wt = [jnp.zeros((8, 128), F32) for _ in range(8)]
    piv = jnp.ones((8, 128), F32)
    for j in range(0, 8, 2):
        a, b, c = _sub(C[j], j), _sub(C[j], j + 1), _sub(C[j + 1], j + 1)
        r = 1.0 / (a * c - b * b)
        i11, i12, i22 = c * r, -b * r, a * r
        ra = 1.0 / a
        e = b * ra
        piv = jnp.where(sub == j, a, jnp.where(sub == j + 1, c - b * e, piv))
        for k in range(j):
            low = C[k] - e * _sub(C[k], j)
            Wt[k] = jnp.where(sub == j, C[k], jnp.where(sub == j + 1, low, Wt[k]))
        Wt[j] = jnp.where(sub == j, 1.0, jnp.where(sub == j + 1, -e, Wt[j]))
        Wt[j + 1] = jnp.where(sub == j + 1, 1.0, Wt[j + 1])
        for k in range(8):
            if k not in (j, j + 1):
                q0, q1 = _sub(C[k], j), _sub(C[k], j + 1)
                s0 = i11 * q0 + i12 * q1
                s1 = i12 * q0 + i22 * q1
                new = C[k] - (C[j] * s0 + C[j + 1] * s1)
                C[k] = jnp.where(sub == j, s0, jnp.where(sub == j + 1, s1, new))
        x, y = C[j], C[j + 1]
        C[j] = jnp.where(sub == j, i11, jnp.where(sub == j + 1, i12, -(x * i11 + y * i12)))
        C[j + 1] = jnp.where(sub == j, i12, jnp.where(sub == j + 1, i22, -(x * i12 + y * i22)))
    rs = lax.rsqrt(piv)
    return C, [w * rs for w in Wt]

def tree(xs):
    xs = list(xs)
    while len(xs) > 1:
        xs = [xs[i] + xs[i + 1] if i + 1 < len(xs) else xs[i] for i in range(0, len(xs), 2)]
    return xs[0]

def invchol128(M, hook):
    n = len(M)
    M = list(M)
    sub = lax.broadcasted_iota(jnp.int32, (8, 128), 0)
    lane = lax.broadcasted_iota(jnp.int32, (8, 128), 1)
    out = []
    for k in range(n):
        hook(k)
        blk = (lane >= 8 * k) & (lane < 8 * k + 8)
        Cb = [[jnp.broadcast_to(M[i][:, 8 * k + u:8 * k + u + 1], (8, 128)) for u in range(8)] for i in range(k, n)]
        m = jnp.where(blk, jnp.where(lane == 8 * k + sub, 1.0, 0.0), M[k])
        mb = [_sub(m, u) for u in range(8)]
        P, W8 = sweep(Cb[0], sub)
        T = tree([P[u] * mb[u] for u in range(8)])
        Tb = [_sub(T, u) for u in range(8)]
        for i in range(k + 1, n):
            M[i] = jnp.where(blk, 0.0, M[i]) - tree([Cb[i - k][u] * Tb[u] for u in range(8)])
        row = tree([W8[u] * mb[u] for u in range(8)])
        out.append(jnp.where(lane < 8 * k + 8, row, 0.0))
    return out

def dot(a, b, dims=((1,), (0,))):
    return lax.dot_general(a, b, (dims, ((), ())), precision=HI, preferred_element_type=F32)

def rows_of(tiles, part):
    return jnp.concatenate([tiles[i, part] for i in range(16)], axis=0)


def inverse_factor(tiles, w, tmp, hook):
    o = invchol128([tiles[i, 0] for i in range(16)], lambda k: hook(0, k))
    for i in range(16):
        w[8 * i:8 * i + 8, 0:128] = o[i]
        w[8 * i:8 * i + 8, 128:256] = jnp.zeros((8, 128), F32)
    w11 = w[0:128, 0:128]
    l21 = dot(rows_of(tiles, 1), w11, ((1,), (1,)))
    s = rows_of(tiles, 2) - dot(l21, l21, ((1,), (1,)))
    tmp[...] = dot(l21, w11)
    o = invchol128([s[8 * i:8 * i + 8] for i in range(16)], lambda k: hook(1, k))
    for i in range(16):
        w[128 + 8 * i:136 + 8 * i, 128:256] = o[i]
    w[128:256, 0:128] = -dot(w[128:256, 128:256], tmp[...])


MESH = pl.DeviceIdType.MESH
NZ, NX, NY = 8, 4, 4
PLANE = NX * NY * 2
CUTS = (0, 1536, 3072, 4352, 5120)
CHUNKS = len(CUTS) - 1


def _wait(view, sem):
    pltpu.make_async_copy(view, view, sem).wait()


def _column(rows):
    r = rows.shape[0]
    return jnp.concatenate([rows, jnp.zeros((128 - r, 128), F32)], axis=0).T


class Ring4:
    def __init__(self, block, i, ids, plus, minus, sems, out):
        self.block, self.plus, self.minus, self.sems, self.out = block, plus, minus, sems, out
        self.i, self.ids = i, ids
        self.up, self.down, self.far = lax.rem(i + 1, 4), lax.rem(i + 3, 4), lax.rem(i + 2, 4)

    def send(self, q, owner, forward, slot):
        buf = self.plus if forward else self.minus
        pltpu.make_async_remote_copy(
            src_ref=self.block(q, owner),
            dst_ref=buf.at[slot],
            send_sem=self.sems.at[6 if forward else 7],
            recv_sem=self.sems.at[slot if forward else 3 + slot],
            device_id=self.ids(self.up if forward else self.down),
            device_id_type=MESH,
        ).start()

    def start(self):
        self.send(0, self.far, True, 0)
        self.send(1, self.far, False, 0)

    def middle(self):
        _wait(self.plus.at[0], self.sems.at[0])
        ref = self.block(0, self.up)
        ref[...] = ref[...] + self.plus[0]
        self.send(0, self.up, True, 2)
        _wait(self.minus.at[0], self.sems.at[3])
        ref = self.block(1, self.down)
        ref[...] = ref[...] + self.minus[0]
        self.send(1, self.down, False, 2)
        self.send(1, self.up, True, 1)
        self.send(0, self.down, False, 1)

    def finish(self):
        for s in (1, 2):
            _wait(self.plus.at[s], self.sems.at[s])
            _wait(self.minus.at[s], self.sems.at[3 + s])
        self.out[0] = self.block(0, self.i)[...] + (self.plus[2] + self.minus[1])
        self.out[1] = self.block(1, self.i)[...] + (self.plus[1] + self.minus[2])

    def drain(self):
        _wait(self.plus, self.sems.at[6])
        _wait(self.minus, self.sems.at[7])


class Ring8:
    def __init__(self, data, z, ids, plus, minus, sems):
        self.data, self.z, self.plus, self.minus, self.sems = data, z, plus, minus, sems
        self.next, self.last = ids(lax.rem(z + 1, 8)), ids(lax.rem(z + 7, 8))

    def send(self, step, src_up, src_down):
        lo, hi = (0, 2) if step == 0 else (4 * step - 2, 4 * step + 2)
        for src, buf, device, side in ((src_up, self.plus, self.next, 0), (src_down, self.minus, self.last, 1)):
            pltpu.make_async_remote_copy(
                src_ref=src, dst_ref=buf.at[lo:hi], send_sem=self.sems.at[8 + side],
                recv_sem=self.sems.at[4 * side + step], device_id=device, device_id_type=MESH).start()

    def start(self):
        far = lax.rem(self.z + 4, 8)
        self.send(0, self.data.at[far, 0:2], self.data.at[far, 2:4])

    def step(self, k):
        lo, hi = (0, 2) if k == 1 else (4 * k - 6, 4 * k - 2)
        up, down = lax.rem(self.z + 4 - k, 8), lax.rem(self.z + 4 + k, 8)
        for buf, at, part, side in ((self.plus, up, slice(0, 2), 0), (self.minus, down, slice(2, 4), 1)):
            _wait(buf.at[lo:hi], self.sems.at[4 * side + k - 1])
            ref = self.data.at[at, part] if k == 1 else self.data.at[at]
            ref[...] = ref[...] + buf[lo:hi]
        self.send(k, self.data.at[up], self.data.at[down])

    def finish(self, out):
        for side, buf in enumerate((self.plus, self.minus)):
            _wait(buf.at[10:14], self.sems.at[4 * side + 3])
        out[...] = self.data[self.z] + (self.plus[10:14] + self.minus[10:14])

    def drain(self):
        _wait(self.plus, self.sems.at[8])
        _wait(self.minus, self.sems.at[9])


def kernel(cells_all, counts, basis, scale, cells, cell_basis, gene_side,
           cbuf, bbuf, sbc, sk, wt, gl, gr, gp, zr, gz, gfull, w, tmp, stg, S, R, SZ, RZ, ZP, ZM, zt, zq,
           XP, XM, YP, YM, PX, PY, X2P, X2M, Y2P, Y2M, Q, zs, z3,
           load_sem, gsem, csem, rsem, zsem, qsem):
    sec = lax.axis_index("section")
    y = lax.axis_index("atlas")
    c = lax.rem(sec, 2)
    x = lax.rem(sec // 2, NX)
    z = sec // (2 * NX)
    h = x * NY + y

    def z_id(k):
        return ((k * NX + x) * 2 + c, y)

    def x_id(k):
        return ((z * NX + k) * 2 + c, y)

    def y_id(k):
        return (sec, k)

    partner = (sec + 1 - 2 * c, y)
    others = []
    for dx in (2, 1, 3, 0):
        for dy in (2, 1, 3, 0):
            if dx or dy:
                px, py = lax.rem(x + dx, NX), lax.rem(y + dy, NY)
                others.append((dx * NY + dy, px * NY + py, [((z * NX + px) * 2 + b, py) for b in range(2)]))

    def put(src, dst, pair, device):
        pltpu.make_async_remote_copy(
            src_ref=src, dst_ref=dst, send_sem=pair.at[0], recv_sem=pair.at[1],
            device_id=device, device_id_type=MESH).start()

    def by_core(fn):
        for b in range(2):
            pl.when(c == b)(functools.partial(fn, b))

    def loads(k):
        cols = slice(CUTS[k], CUTS[k + 1])
        return (pltpu.make_async_copy(counts.at[:, cols], cbuf.at[:, cols], load_sem.at[0, k]),
                pltpu.make_async_copy(basis.at[cols, :], bbuf.at[cols, :], load_sem.at[1, k]))

    for k in range(CHUNKS):
        for copy in loads(k):
            copy.start()

    barrier = pltpu.get_barrier_semaphore()
    for _, _, ids in others:
        for device in ids:
            pl.semaphore_signal(barrier, inc=1, device_id=device, device_id_type=MESH)
    pl.semaphore_signal(barrier, inc=1, device_id=partner, device_id_type=MESH)

    @pl.loop(1, NZ)
    def _(d):
        pl.semaphore_signal(barrier, inc=1, device_id=z_id(lax.rem(z + d, NZ)), device_id_type=MESH)

    turned = _column(scale[...])
    for g in range(scale.shape[0]):
        sbc[128 * g:128 * g + 128, :] = jnp.broadcast_to(turned[:, g:g + 1], (128, 128))
    for k in range(CHUNKS):
        for copy in loads(k):
            copy.wait()
        rows = slice(CUTS[k], CUTS[k + 1])
        factor = sbc[rows, :]
        part = bbuf[rows, :].astype(F32)
        scaled = jnp.concatenate([part[:, :128] * factor, part[:, 128:] * factor], axis=1).astype(jnp.bfloat16)
        term = jnp.dot(cbuf[:, rows], scaled, preferred_element_type=F32)
        sk[...] = term if k == 0 else sk[...] + term

    turned = _column(cells[...])
    for r in range(cells.shape[0]):
        rows = slice(128 * r, 128 * r + 128)
        factor = jnp.broadcast_to(turned[:, r:r + 1], (128, 256))
        value = sk[rows, :] * factor
        sk[rows, :] = value
        wt[rows, :] = (value * factor).astype(jnp.bfloat16)

    gram = dot(sk[...], sk[...], ((0,), (0,))) * (1.0 / cells_all)
    for i in range(16):
        gl[i, 0] = gram[8 * i:8 * i + 8, :128]
        gl[i, 1] = gram[128 + 8 * i:136 + 8 * i, :128]
        gl[i, 2] = gram[128 + 8 * i:136 + 8 * i, 128:]

    pl.semaphore_wait(barrier, PLANE - 1 + NZ - 1)

    for r, chip, ids in others:
        place = (2 * r + c) * 2
        put(gl.at[chip, 0:1], gr.at[pl.ds(place, 1)], gsem.at[0], ids[0])
        put(gl.at[chip, 1:3], gr.at[pl.ds(place, 2)], gsem.at[0], ids[1])

    def to_partner(b):
        n = 2 - b
        put(gl.at[h, 1 - b:1 - b + n], gr.at[2 * b:2 * b + n], gsem.at[0], partner)
        gr[2 * b] = gl[h, b]
        gr[2 * b + 1] = gl[h, 2 * b]

    by_core(to_partner)

    def sums(batch, begin, end):
        @pl.loop(begin, end)
        def _(j):
            cols = pl.ds(pl.multiple_of((2 * j + batch) * 640, 128), 640)
            part = lax.dot_general(cbuf[:, cols], wt[...], (((0,), (0,)), ((), ())), preferred_element_type=F32)
            factor = sbc[cols, :] * (1.0 / cells_all)
            stg[:, :128] = part[:, :128] * factor
            stg[:, 128:] = part[:, 128:] * factor
            for a in range(NX):
                for b in range(2):
                    for e in range(NY):
                        o = ((a * 2 + b) * NY + e) * 20
                        S[b, batch, 0, j, a, e] = stg[o:o + 8, :128]
                        S[b, batch, 1, j, a, e] = stg[o:o + 8, 128:]
                        S[b, batch, 2, j, a, e] = stg[o + 8:o + 16, :128]
                        S[b, batch, 3, j, a, e] = stg[o + 8:o + 16, 128:]
                        SZ[b, 2 * j + batch, a, e] = jnp.concatenate(
                            [stg[o + 16:o + 20, :128], stg[o + 16:o + 20, 128:]], axis=0)
            put(S.at[1 - c, batch, :, j], R.at[batch, :, j], csem.at[batch], partner)
            put(SZ.at[1 - c, 2 * j + batch], RZ.at[2 * j + batch], csem.at[2], partner)

    sums(0, 0, 4)
    sums(1, 0, 2)

    first, second, third, fourth = [], [], [], []
    for batch in range(2):
        first.append(Ring4(lambda q, o, n=batch: R.at[n, q, :, o], x, x_id,
                           XP.at[batch], XM.at[batch], rsem.at[batch, 0], PX.at[batch]))
        second.append(Ring4(lambda q, o, n=batch: R.at[n, 2 + q, :, :, o], y, y_id,
                            YP.at[batch], YM.at[batch], rsem.at[batch, 1], PY.at[batch]))
        third.append(Ring4(lambda q, o, n=batch: PX.at[n, q, :, o], y, y_id,
                           X2P.at[batch], X2M.at[batch], rsem.at[batch, 2], Q.at[batch, 0:2]))
        fourth.append(Ring4(lambda q, o, n=batch: PY.at[n, q, :, o], x, x_id,
                            Y2P.at[batch], Y2M.at[batch], rsem.at[batch, 3], Q.at[batch, 2:4]))

    def add_partner(batch):
        _wait(R.at[batch], csem.at[batch, 1])

        @pl.loop(0, 4)
        def _(u):
            for q in range(4):
                R[batch, q, u] = R[batch, q, u] + S[c, batch, q, u]

    def stage_one(batch):
        first[batch].start()
        second[batch].start()

    def stage_one_middle(batch):
        first[batch].middle()
        second[batch].middle()

    def stage_two(batch):
        first[batch].finish()
        third[batch].start()
        second[batch].finish()
        fourth[batch].start()

    def stage_two_middle(batch):
        third[batch].middle()
        fourth[batch].middle()

    def stage_three(batch):
        third[batch].finish()
        fourth[batch].finish()
        for j in range(NZ // 2):
            k = 2 * j + batch
            for t in range(4):
                zs[k, t] = Q[batch, t, j]
            d = lax.rem(k - z + NZ, NZ)

            @pl.when(d > 0)
            def _():
                put(zs.at[k], z3.at[d - 1], zsem, z_id(k))

    over = Ring8(RZ, z, z_id, ZP, ZM, qsem)

    def z_start():
        _wait(RZ, csem.at[2, 1])

        @pl.loop(0, NZ)
        def _(k):
            RZ[k] = RZ[k] + SZ[c, k]

        over.start()

    def z_finish():
        over.finish(zt)
        zq[0] = zt[x, y]
        for r, chip, ids in others:
            pltpu.make_async_remote_copy(
                src_ref=zt.at[chip // NY, lax.rem(chip, NY)], dst_ref=zq.at[r], send_sem=qsem.at[10], recv_sem=qsem.at[11],
                device_id=(ids[0][0] + c, ids[0][1]), device_id_type=MESH).start()

    add_partner(0)
    stage_one(0)
    sums(1, 2, 4)

    by_core(lambda b: _wait(gr.at[0:31 * (b + 1)], gsem.at[0, 1]))
    gp[...] = jnp.sum(gr[...].reshape(PLANE, 2, 8, 128), axis=0)

    def over_z(b):
        @pl.loop(1, NZ)
        def _(d):
            put(gp.at[0:b + 1], zr.at[pl.ds(2 * (d - 1), b + 1)], gsem.at[1], z_id(lax.rem(z + d, NZ)))

    by_core(over_z)

    add_partner(1)
    z_start()

    stage_one_middle(0)

    by_core(lambda b: _wait(zr.at[0:7 * (b + 1)], gsem.at[1, 1]))
    gz[...] = gp[...] + jnp.sum(zr[...].reshape(NZ - 1, 2, 8, 128), axis=0)

    def spread(b):
        n = b + 1
        gfull[h, b] = gz[0]
        if b:
            gfull[h, 2] = gz[1]
        for _, _, ids in others:
            put(gz.at[0:n], gfull.at[h, b:b + n], gsem.at[2], ids[b])

    by_core(spread)

    stage_one(1)
    over.step(1)

    def hand_over(b):
        n = b + 1
        _wait(gr.at[0:15 * n], gsem.at[2, 1])
        put(gfull.at[:, b:b + n], gfull.at[:, b:b + n], gsem.at[3], partner)

    by_core(hand_over)
    stage_two(0)
    over.step(2)
    stage_one_middle(1)
    by_core(lambda b: _wait(gr.at[0:16 * (2 - b)], gsem.at[3, 1]))

    events = {
        (0, 2): lambda: over.step(3),
        (0, 4): lambda: stage_two_middle(0),
        (0, 10): lambda: stage_three(0),
        (0, 13): z_finish,
        (0, 15): lambda: stage_two(1),
        (1, 2): lambda: stage_two_middle(1),
        (1, 9): lambda: stage_three(1),
    }

    def hook(half, k):
        if (half, k) in events:
            with jax.named_scope(f"e{half}_{k}"):
                events[half, k]()

    inverse_factor(gfull, w, tmp, hook)

    cell_basis[...] = dot(sk[...], w[...], ((1,), (1,))).astype(jnp.bfloat16)

    _wait(z3, zsem.at[1])
    _wait(zq.at[1:16], qsem.at[11])
    own = zs[z] + jnp.sum(z3[...], axis=0)
    top = jnp.concatenate([own[0], own[1]], axis=1)
    mid = jnp.concatenate([own[2], own[3]], axis=1)
    rest = jnp.sum(zq[...], axis=0)
    low = jnp.concatenate([rest, pltpu.roll(rest, 4, 0)], axis=1)
    side = dot(jnp.concatenate([top, mid, low], axis=0), w[...], ((1,), (1,)))
    gene_side[...] = side[:20]

    def drain(b):
        _wait(gr.at[0:47 - b], gsem.at[0, 0])
        _wait(zr.at[0:7 * (b + 1)], gsem.at[1, 0])
        _wait(gr.at[0:15 * (b + 1)], gsem.at[2, 0])
        _wait(gr.at[0:16 * (b + 1)], gsem.at[3, 0])

    by_core(drain)
    for batch in range(2):
        _wait(R.at[batch], csem.at[batch, 0])
        for ring in (first[batch], second[batch], third[batch], fourth[batch]):
            ring.drain()
    _wait(z3, zsem.at[0])
    _wait(RZ, csem.at[2, 0])
    over.drain()
    _wait(zq.at[1:16], qsem.at[10])


def hand_on(a, b, a_out, b_out):
    a_out[...] = a[...]
    b_out[...] = b[...]


def local(counts, gene_scale, cell_scale, gene_basis):
    device_count = lax.axis_size("section") * lax.axis_size("atlas")
    rows, genes = counts.shape
    vm = lambda *s: pltpu.VMEM(s, F32)
    dma = pltpu.SemaphoreType.DMA
    shapes = (jax.ShapeDtypeStruct((rows, 256), jnp.bfloat16),
              jax.ShapeDtypeStruct((genes // device_count, 256), F32))
    result = pl.pallas_call(
        functools.partial(kernel, rows * device_count),
        out_shape=shapes,
        in_specs=[pl.BlockSpec(memory_space=pl.ANY)] * 2 + [pl.BlockSpec(memory_space=pltpu.VMEM)] * 2,
        out_specs=(pl.BlockSpec(memory_space=pltpu.VMEM),) * 2,
        scratch_shapes=[
            pltpu.VMEM((rows, genes), jnp.bfloat16), pltpu.VMEM((genes, 256), jnp.bfloat16),
            vm(genes, 128), vm(rows, 256), pltpu.VMEM((rows, 256), jnp.bfloat16),
            vm(16, 3, 8, 128), vm(64, 8, 128), vm(2, 8, 128), vm(14, 8, 128), vm(2, 8, 128),
            vm(16, 3, 8, 128), vm(256, 256), vm(128, 128), vm(640, 256),
            vm(2, 2, 4, 4, NX, NY, 8, 128), vm(2, 4, 4, NX, NY, 8, 128),
            vm(2, NZ, NX, NY, 8, 128), vm(NZ, NX, NY, 8, 128), vm(14, NY, 8, 128), vm(14, NY, 8, 128),
            vm(NX, NY, 8, 128), vm(NX * NY, 8, 128),
            vm(2, 3, 4, 4, 8, 128), vm(2, 3, 4, 4, 8, 128), vm(2, 3, 4, 4, 8, 128), vm(2, 3, 4, 4, 8, 128),
            vm(2, 2, 4, 4, 8, 128), vm(2, 2, 4, 4, 8, 128),
            vm(2, 3, 4, 8, 128), vm(2, 3, 4, 8, 128), vm(2, 3, 4, 8, 128), vm(2, 3, 4, 8, 128),
            vm(2, 4, 4, 8, 128), vm(NZ, 4, 8, 128), vm(NZ - 1, 4, 8, 128),
            dma((2, CHUNKS)), dma((4, 2)), dma((3, 2)), dma((2, 4, 8)), dma((2,)), dma((12,)),
        ],
        compiler_params=pltpu.CompilerParams(collective_id=0, has_side_effects=True, vmem_limit_bytes=60 << 20),
    )(counts, gene_basis, gene_scale.reshape(genes // 128, 128), cell_scale.reshape(rows // 128, 128))
    return pl.pallas_call(hand_on, out_shape=shapes)(*result)


def solution(mesh):
    return jax.shard_map(
        local,
        mesh=mesh,
        in_specs=(P(("section", "atlas"), None), P(), P(("section", "atlas")), P()),
        out_specs=(P(("section", "atlas"), None), P(("section", "atlas"), None)),
        check_vma=False,
    )
```

```python
import functools

import jax
import jax.numpy as jnp
from jax import lax
from jax.experimental import pallas as pl
from jax.experimental.pallas import tpu as pltpu
from jax.sharding import PartitionSpec as P

HI = lax.Precision.HIGHEST
F32 = jnp.float32

def _sub(x, j):
    return jnp.broadcast_to(x[j:j + 1, :], x.shape)

def sweep(C, sub):
    C = list(C)
    Wt = [jnp.zeros((8, 128), F32) for _ in range(8)]
    piv = jnp.ones((8, 128), F32)
    for j in range(0, 8, 2):
        a, b, c = _sub(C[j], j), _sub(C[j], j + 1), _sub(C[j + 1], j + 1)
        r = 1.0 / (a * c - b * b)
        i11, i12, i22 = c * r, -b * r, a * r
        ra = 1.0 / a
        e = b * ra
        piv = jnp.where(sub == j, a, jnp.where(sub == j + 1, c - b * e, piv))
        for k in range(j):
            low = C[k] - e * _sub(C[k], j)
            Wt[k] = jnp.where(sub == j, C[k], jnp.where(sub == j + 1, low, Wt[k]))
        Wt[j] = jnp.where(sub == j, 1.0, jnp.where(sub == j + 1, -e, Wt[j]))
        Wt[j + 1] = jnp.where(sub == j + 1, 1.0, Wt[j + 1])
        for k in range(8):
            if k not in (j, j + 1):
                q0, q1 = _sub(C[k], j), _sub(C[k], j + 1)
                s0 = i11 * q0 + i12 * q1
                s1 = i12 * q0 + i22 * q1
                new = C[k] - (C[j] * s0 + C[j + 1] * s1)
                C[k] = jnp.where(sub == j, s0, jnp.where(sub == j + 1, s1, new))
        x, y = C[j], C[j + 1]
        C[j] = jnp.where(sub == j, i11, jnp.where(sub == j + 1, i12, -(x * i11 + y * i12)))
        C[j + 1] = jnp.where(sub == j, i12, jnp.where(sub == j + 1, i22, -(x * i12 + y * i22)))
    rs = lax.rsqrt(piv)
    return C, [w * rs for w in Wt]

def tree(xs):
    xs = list(xs)
    while len(xs) > 1:
        xs = [xs[i] + xs[i + 1] if i + 1 < len(xs) else xs[i] for i in range(0, len(xs), 2)]
    return xs[0]

def invchol128(M, hook):
    n = len(M)
    M = list(M)
    sub = lax.broadcasted_iota(jnp.int32, (8, 128), 0)
    lane = lax.broadcasted_iota(jnp.int32, (8, 128), 1)
    out = []
    for k in range(n):
        hook(k)
        blk = (lane >= 8 * k) & (lane < 8 * k + 8)
        Cb = [[jnp.broadcast_to(M[i][:, 8 * k + u:8 * k + u + 1], (8, 128)) for u in range(8)] for i in range(k, n)]
        m = jnp.where(blk, jnp.where(lane == 8 * k + sub, 1.0, 0.0), M[k])
        mb = [_sub(m, u) for u in range(8)]
        P, W8 = sweep(Cb[0], sub)
        T = tree([P[u] * mb[u] for u in range(8)])
        Tb = [_sub(T, u) for u in range(8)]
        for i in range(k + 1, n):
            M[i] = jnp.where(blk, 0.0, M[i]) - tree([Cb[i - k][u] * Tb[u] for u in range(8)])
        row = tree([W8[u] * mb[u] for u in range(8)])
        out.append(jnp.where(lane < 8 * k + 8, row, 0.0))
    return out

def dot(a, b, dims=((1,), (0,))):
    return lax.dot_general(a, b, (dims, ((), ())), precision=HI, preferred_element_type=F32)

def rows_of(tiles, part):
    return jnp.concatenate([tiles[i, part] for i in range(16)], axis=0)


def inverse_factor(tiles, w, tmp, hook):
    o = invchol128([tiles[i, 0] for i in range(16)], lambda k: hook(0, k))
    for i in range(16):
        w[8 * i:8 * i + 8, 0:128] = o[i]
        w[8 * i:8 * i + 8, 128:256] = jnp.zeros((8, 128), F32)
    w11 = w[0:128, 0:128]
    l21 = dot(rows_of(tiles, 1), w11, ((1,), (1,)))
    s = rows_of(tiles, 2) - dot(l21, l21, ((1,), (1,)))
    tmp[...] = dot(l21, w11)
    o = invchol128([s[8 * i:8 * i + 8] for i in range(16)], lambda k: hook(1, k))
    for i in range(16):
        w[128 + 8 * i:136 + 8 * i, 128:256] = o[i]
    w[128:256, 0:128] = -dot(w[128:256, 128:256], tmp[...])


MESH = pl.DeviceIdType.MESH
NZ, NX, NY = 8, 4, 4
PLANE = NX * NY * 2
CUTS = (0, 1536, 3072, 4352, 5120)
CHUNKS = len(CUTS) - 1


def _wait(view, sem):
    pltpu.make_async_copy(view, view, sem).wait()


def _column(rows):
    r = rows.shape[0]
    return jnp.concatenate([rows, jnp.zeros((128 - r, 128), F32)], axis=0).T


class Ring4:
    def __init__(self, block, i, ids, plus, minus, sems, out):
        self.block, self.plus, self.minus, self.sems, self.out = block, plus, minus, sems, out
        self.i, self.ids = i, ids
        self.up, self.down, self.far = lax.rem(i + 1, 4), lax.rem(i + 3, 4), lax.rem(i + 2, 4)

    def send(self, q, owner, forward, slot):
        buf = self.plus if forward else self.minus
        pltpu.make_async_remote_copy(
            src_ref=self.block(q, owner),
            dst_ref=buf.at[slot],
            send_sem=self.sems.at[6 if forward else 7],
            recv_sem=self.sems.at[slot if forward else 3 + slot],
            device_id=self.ids(self.up if forward else self.down),
            device_id_type=MESH,
        ).start()

    def start(self):
        self.send(0, self.far, True, 0)
        self.send(1, self.far, False, 0)

    def middle(self):
        _wait(self.plus.at[0], self.sems.at[0])
        ref = self.block(0, self.up)
        ref[...] = ref[...] + self.plus[0]
        self.send(0, self.up, True, 2)
        _wait(self.minus.at[0], self.sems.at[3])
        ref = self.block(1, self.down)
        ref[...] = ref[...] + self.minus[0]
        self.send(1, self.down, False, 2)
        self.send(1, self.up, True, 1)
        self.send(0, self.down, False, 1)

    def finish(self):
        for s in (1, 2):
            _wait(self.plus.at[s], self.sems.at[s])
            _wait(self.minus.at[s], self.sems.at[3 + s])
        self.out[0] = self.block(0, self.i)[...] + (self.plus[2] + self.minus[1])
        self.out[1] = self.block(1, self.i)[...] + (self.plus[1] + self.minus[2])

    def drain(self):
        _wait(self.plus, self.sems.at[6])
        _wait(self.minus, self.sems.at[7])


class Ring8:
    def __init__(self, data, z, ids, plus, minus, sems):
        self.data, self.z, self.plus, self.minus, self.sems = data, z, plus, minus, sems
        self.next, self.last = ids(lax.rem(z + 1, 8)), ids(lax.rem(z + 7, 8))

    def send(self, step, src_up, src_down):
        lo, hi = (0, 2) if step == 0 else (4 * step - 2, 4 * step + 2)
        for src, buf, device, side in ((src_up, self.plus, self.next, 0), (src_down, self.minus, self.last, 1)):
            pltpu.make_async_remote_copy(
                src_ref=src, dst_ref=buf.at[lo:hi], send_sem=self.sems.at[8 + side],
                recv_sem=self.sems.at[4 * side + step], device_id=device, device_id_type=MESH).start()

    def start(self):
        far = lax.rem(self.z + 4, 8)
        self.send(0, self.data.at[far, 0:2], self.data.at[far, 2:4])

    def step(self, k):
        lo, hi = (0, 2) if k == 1 else (4 * k - 6, 4 * k - 2)
        up, down = lax.rem(self.z + 4 - k, 8), lax.rem(self.z + 4 + k, 8)
        for buf, at, part, side in ((self.plus, up, slice(0, 2), 0), (self.minus, down, slice(2, 4), 1)):
            _wait(buf.at[lo:hi], self.sems.at[4 * side + k - 1])
            ref = self.data.at[at, part] if k == 1 else self.data.at[at]
            ref[...] = ref[...] + buf[lo:hi]
        self.send(k, self.data.at[up], self.data.at[down])

    def finish(self, out):
        for side, buf in enumerate((self.plus, self.minus)):
            _wait(buf.at[10:14], self.sems.at[4 * side + 3])
        out[...] = self.data[self.z] + (self.plus[10:14] + self.minus[10:14])

    def drain(self):
        _wait(self.plus, self.sems.at[8])
        _wait(self.minus, self.sems.at[9])


def kernel(cells_all, counts, basis, scale, cells, cell_basis, gene_side,
           cbuf, bbuf, sbc, sk, wt, gl, gr, gp, zr, gz, gfull, w, tmp, stg, S, R, SZ, RZ, ZP, ZM, zt, zq,
           XP, XM, YP, YM, PX, PY, X2P, X2M, Y2P, Y2M, Q, zs, z3,
           load_sem, gsem, csem, rsem, zsem, qsem):
    sec = lax.axis_index("section")
    y = lax.axis_index("atlas")
    c = lax.rem(sec, 2)
    x = lax.rem(sec // 2, NX)
    z = sec // (2 * NX)
    h = x * NY + y

    def z_id(k):
        return ((k * NX + x) * 2 + c, y)

    def x_id(k):
        return ((z * NX + k) * 2 + c, y)

    def y_id(k):
        return (sec, k)

    partner = (sec + 1 - 2 * c, y)
    others = []
    for dx in (2, 1, 3, 0):
        for dy in (2, 1, 3, 0):
            if dx or dy:
                px, py = lax.rem(x + dx, NX), lax.rem(y + dy, NY)
                others.append((dx * NY + dy, px * NY + py, [((z * NX + px) * 2 + b, py) for b in range(2)]))

    def put(src, dst, pair, device):
        pltpu.make_async_remote_copy(
            src_ref=src, dst_ref=dst, send_sem=pair.at[0], recv_sem=pair.at[1],
            device_id=device, device_id_type=MESH).start()

    def by_core(fn):
        for b in range(2):
            pl.when(c == b)(functools.partial(fn, b))

    def alone(fn):
        pl.when(sec >= 0)(fn)

    def loads(k):
        cols = slice(CUTS[k], CUTS[k + 1])
        return (pltpu.make_async_copy(counts.at[:, cols], cbuf.at[:, cols], load_sem.at[0, k]),
                pltpu.make_async_copy(basis.at[cols, :], bbuf.at[cols, :], load_sem.at[1, k]))

    @alone
    def _():
        for k in range(CHUNKS):
            for copy in loads(k):
                copy.start()

    barrier = pltpu.get_barrier_semaphore()
    for _, _, ids in others:
        for device in ids:
            pl.semaphore_signal(barrier, inc=1, device_id=device, device_id_type=MESH)
    pl.semaphore_signal(barrier, inc=1, device_id=partner, device_id_type=MESH)

    @pl.loop(1, NZ)
    def _(d):
        pl.semaphore_signal(barrier, inc=1, device_id=z_id(lax.rem(z + d, NZ)), device_id_type=MESH)

    turned = _column(scale[...])
    for g in range(scale.shape[0]):
        sbc[128 * g:128 * g + 128, :] = jnp.broadcast_to(turned[:, g:g + 1], (128, 128))
    for k in range(CHUNKS):
        for copy in loads(k):
            copy.wait()
        rows = slice(CUTS[k], CUTS[k + 1])
        factor = sbc[rows, :]
        part = bbuf[rows, :].astype(F32)
        scaled = jnp.concatenate([part[:, :128] * factor, part[:, 128:] * factor], axis=1).astype(jnp.bfloat16)
        term = jnp.dot(cbuf[:, rows], scaled, preferred_element_type=F32)
        sk[...] = term if k == 0 else sk[...] + term

    turned = _column(cells[...])
    for r in range(cells.shape[0]):
        rows = slice(128 * r, 128 * r + 128)
        factor = jnp.broadcast_to(turned[:, r:r + 1], (128, 256))
        value = sk[rows, :] * factor
        sk[rows, :] = value
        wt[rows, :] = (value * factor).astype(jnp.bfloat16)

    gram = dot(sk[...], sk[...], ((0,), (0,))) * (1.0 / cells_all)
    for i in range(16):
        gl[i, 0] = gram[8 * i:8 * i + 8, :128]
        gl[i, 1] = gram[128 + 8 * i:136 + 8 * i, :128]
        gl[i, 2] = gram[128 + 8 * i:136 + 8 * i, 128:]

    pl.semaphore_wait(barrier, PLANE - 1 + NZ - 1)

    for r, chip, ids in others:
        place = (2 * r + c) * 2
        put(gl.at[chip, 0:1], gr.at[pl.ds(place, 1)], gsem.at[0], ids[0])
        put(gl.at[chip, 1:3], gr.at[pl.ds(place, 2)], gsem.at[0], ids[1])

    def to_partner(b):
        n = 2 - b
        put(gl.at[h, 1 - b:1 - b + n], gr.at[2 * b:2 * b + n], gsem.at[0], partner)
        gr[2 * b] = gl[h, b]
        gr[2 * b + 1] = gl[h, 2 * b]

    by_core(to_partner)

    def sums(batch, begin, end):
        @pl.loop(begin, end)
        def _(j):
            cols = pl.ds(pl.multiple_of((2 * j + batch) * 640, 128), 640)
            part = lax.dot_general(cbuf[:, cols], wt[...], (((0,), (0,)), ((), ())), preferred_element_type=F32)
            factor = sbc[cols, :] * (1.0 / cells_all)
            stg[:, :128] = part[:, :128] * factor
            stg[:, 128:] = part[:, 128:] * factor
            for a in range(NX):
                for b in range(2):
                    for e in range(NY):
                        o = ((a * 2 + b) * NY + e) * 20
                        S[b, batch, 0, j, a, e] = stg[o:o + 8, :128]
                        S[b, batch, 1, j, a, e] = stg[o:o + 8, 128:]
                        S[b, batch, 2, j, a, e] = stg[o + 8:o + 16, :128]
                        S[b, batch, 3, j, a, e] = stg[o + 8:o + 16, 128:]
                        SZ[b, 2 * j + batch, a, e] = jnp.concatenate(
                            [stg[o + 16:o + 20, :128], stg[o + 16:o + 20, 128:]], axis=0)
            put(S.at[1 - c, batch, :, j], R.at[batch, :, j], csem.at[batch], partner)
            put(SZ.at[1 - c, 2 * j + batch], RZ.at[2 * j + batch], csem.at[2], partner)

    sums(0, 0, 4)
    sums(1, 0, 2)

    first, second, third, fourth = [], [], [], []
    for batch in range(2):
        first.append(Ring4(lambda q, o, n=batch: R.at[n, q, :, o], x, x_id,
                           XP.at[batch], XM.at[batch], rsem.at[batch, 0], PX.at[batch]))
        second.append(Ring4(lambda q, o, n=batch: R.at[n, 2 + q, :, :, o], y, y_id,
                            YP.at[batch], YM.at[batch], rsem.at[batch, 1], PY.at[batch]))
        third.append(Ring4(lambda q, o, n=batch: PX.at[n, q, :, o], y, y_id,
                           X2P.at[batch], X2M.at[batch], rsem.at[batch, 2], Q.at[batch, 0:2]))
        fourth.append(Ring4(lambda q, o, n=batch: PY.at[n, q, :, o], x, x_id,
                            Y2P.at[batch], Y2M.at[batch], rsem.at[batch, 3], Q.at[batch, 2:4]))

    def add_partner(batch):
        _wait(R.at[batch], csem.at[batch, 1])

        @pl.loop(0, 4)
        def _(u):
            for q in range(4):
                R[batch, q, u] = R[batch, q, u] + S[c, batch, q, u]

    def stage_one(batch):
        first[batch].start()
        second[batch].start()

    def stage_one_middle(batch):
        first[batch].middle()
        second[batch].middle()

    def stage_two(batch):
        first[batch].finish()
        third[batch].start()
        second[batch].finish()
        fourth[batch].start()

    def stage_two_middle(batch):
        third[batch].middle()
        fourth[batch].middle()

    def stage_three(batch):
        third[batch].finish()
        fourth[batch].finish()
        for j in range(NZ // 2):
            k = 2 * j + batch
            for t in range(4):
                zs[k, t] = Q[batch, t, j]
            d = lax.rem(k - z + NZ, NZ)

            @pl.when(d > 0)
            def _():
                put(zs.at[k], z3.at[d - 1], zsem, z_id(k))

    over = Ring8(RZ, z, z_id, ZP, ZM, qsem)

    def z_start():
        _wait(RZ, csem.at[2, 1])

        @pl.loop(0, NZ)
        def _(k):
            RZ[k] = RZ[k] + SZ[c, k]

        over.start()

    def z_finish():
        over.finish(zt)
        zq[0] = zt[x, y]
        for r, chip, ids in others:
            pltpu.make_async_remote_copy(
                src_ref=zt.at[chip // NY, lax.rem(chip, NY)], dst_ref=zq.at[r], send_sem=qsem.at[10], recv_sem=qsem.at[11],
                device_id=(ids[0][0] + c, ids[0][1]), device_id_type=MESH).start()

    add_partner(0)
    alone(lambda: stage_one(0))
    sums(1, 2, 4)

    by_core(lambda b: _wait(gr.at[0:31 * (b + 1)], gsem.at[0, 1]))
    gp[...] = jnp.sum(gr[...].reshape(PLANE, 2, 8, 128), axis=0)

    def over_z(b):
        @pl.loop(1, NZ)
        def _(d):
            put(gp.at[0:b + 1], zr.at[pl.ds(2 * (d - 1), b + 1)], gsem.at[1], z_id(lax.rem(z + d, NZ)))

    by_core(over_z)

    add_partner(1)
    alone(z_start)
    alone(lambda: stage_one(1))

    alone(lambda: stage_one_middle(0))

    by_core(lambda b: _wait(zr.at[0:7 * (b + 1)], gsem.at[1, 1]))
    gz[...] = gp[...] + jnp.sum(zr[...].reshape(NZ - 1, 2, 8, 128), axis=0)

    def spread(b):
        n = b + 1
        gfull[h, b] = gz[0]
        if b:
            gfull[h, 2] = gz[1]
        for _, _, ids in others:
            put(gz.at[0:n], gfull.at[h, b:b + n], gsem.at[2], ids[b])

    by_core(spread)

    alone(lambda: over.step(1))
    alone(lambda: stage_one_middle(1))
    alone(lambda: stage_two(0))
    alone(lambda: over.step(2))

    def hand_over(b):
        n = b + 1
        _wait(gr.at[0:15 * n], gsem.at[2, 1])
        put(gfull.at[:, b:b + n], gfull.at[:, b:b + n], gsem.at[3], partner)

    by_core(hand_over)
    by_core(lambda b: _wait(gr.at[0:16 * (2 - b)], gsem.at[3, 1]))

    events = {
        (0, 2): lambda: stage_two(1),
        (0, 5): lambda: stage_two_middle(0),
        (0, 8): lambda: over.step(3),
        (0, 11): lambda: stage_two_middle(1),
        (0, 14): lambda: stage_three(0),
        (1, 2): z_finish,
        (1, 5): lambda: stage_three(1),
    }

    def hook(half, k):
        if (half, k) in events:
            with jax.named_scope(f"e{half}_{k}"):
                alone(events[half, k])

    inverse_factor(gfull, w, tmp, hook)

    cell_basis[...] = dot(sk[...], w[...], ((1,), (1,))).astype(jnp.bfloat16)

    _wait(z3, zsem.at[1])
    _wait(zq.at[1:16], qsem.at[11])
    own = zs[z] + jnp.sum(z3[...], axis=0)
    top = jnp.concatenate([own[0], own[1]], axis=1)
    mid = jnp.concatenate([own[2], own[3]], axis=1)
    rest = jnp.sum(zq[...], axis=0)
    low = jnp.concatenate([rest, pltpu.roll(rest, 4, 0)], axis=1)
    side = dot(jnp.concatenate([top, mid, low], axis=0), w[...], ((1,), (1,)))
    gene_side[...] = side[:20]

    def drain(b):
        _wait(gr.at[0:47 - b], gsem.at[0, 0])
        _wait(zr.at[0:7 * (b + 1)], gsem.at[1, 0])
        _wait(gr.at[0:15 * (b + 1)], gsem.at[2, 0])
        _wait(gr.at[0:16 * (b + 1)], gsem.at[3, 0])

    by_core(drain)
    for batch in range(2):
        _wait(R.at[batch], csem.at[batch, 0])
        for ring in (first[batch], second[batch], third[batch], fourth[batch]):
            ring.drain()
    _wait(z3, zsem.at[0])
    _wait(RZ, csem.at[2, 0])
    over.drain()
    _wait(zq.at[1:16], qsem.at[10])


def hand_on(a, b, a_out, b_out):
    a_out[...] = a[...]
    b_out[...] = b[...]


def local(counts, gene_scale, cell_scale, gene_basis):
    device_count = lax.axis_size("section") * lax.axis_size("atlas")
    rows, genes = counts.shape
    vm = lambda *s: pltpu.VMEM(s, F32)
    dma = pltpu.SemaphoreType.DMA
    shapes = (jax.ShapeDtypeStruct((rows, 256), jnp.bfloat16),
              jax.ShapeDtypeStruct((genes // device_count, 256), F32))
    result = pl.pallas_call(
        functools.partial(kernel, rows * device_count),
        out_shape=shapes,
        in_specs=[pl.BlockSpec(memory_space=pl.ANY)] * 2 + [pl.BlockSpec(memory_space=pltpu.VMEM)] * 2,
        out_specs=(pl.BlockSpec(memory_space=pltpu.VMEM),) * 2,
        scratch_shapes=[
            pltpu.VMEM((rows, genes), jnp.bfloat16), pltpu.VMEM((genes, 256), jnp.bfloat16),
            vm(genes, 128), vm(rows, 256), pltpu.VMEM((rows, 256), jnp.bfloat16),
            vm(16, 3, 8, 128), vm(64, 8, 128), vm(2, 8, 128), vm(14, 8, 128), vm(2, 8, 128),
            vm(16, 3, 8, 128), vm(256, 256), vm(128, 128), vm(640, 256),
            vm(2, 2, 4, 4, NX, NY, 8, 128), vm(2, 4, 4, NX, NY, 8, 128),
            vm(2, NZ, NX, NY, 8, 128), vm(NZ, NX, NY, 8, 128), vm(14, NY, 8, 128), vm(14, NY, 8, 128),
            vm(NX, NY, 8, 128), vm(NX * NY, 8, 128),
            vm(2, 3, 4, 4, 8, 128), vm(2, 3, 4, 4, 8, 128), vm(2, 3, 4, 4, 8, 128), vm(2, 3, 4, 4, 8, 128),
            vm(2, 2, 4, 4, 8, 128), vm(2, 2, 4, 4, 8, 128),
            vm(2, 3, 4, 8, 128), vm(2, 3, 4, 8, 128), vm(2, 3, 4, 8, 128), vm(2, 3, 4, 8, 128),
            vm(2, 4, 4, 8, 128), vm(NZ, 4, 8, 128), vm(NZ - 1, 4, 8, 128),
            dma((2, CHUNKS)), dma((4, 2)), dma((3, 2)), dma((2, 4, 8)), dma((2,)), dma((12,)),
        ],
        compiler_params=pltpu.CompilerParams(collective_id=0, has_side_effects=True, vmem_limit_bytes=60 << 20),
    )(counts, gene_basis, gene_scale.reshape(genes // 128, 128), cell_scale.reshape(rows // 128, 128))
    return pl.pallas_call(hand_on, out_shape=shapes)(*result)


def solution(mesh):
    return jax.shard_map(
        local,
        mesh=mesh,
        in_specs=(P(("section", "atlas"), None), P(), P(("section", "atlas")), P()),
        out_specs=(P(("section", "atlas"), None), P(("section", "atlas"), None)),
        check_vma=False,
    )
```

```python
import functools

import jax
import jax.numpy as jnp
from jax import lax
from jax.experimental import pallas as pl
from jax.experimental.pallas import tpu as pltpu
from jax.sharding import PartitionSpec as P

HI = lax.Precision.HIGHEST
F32 = jnp.float32

def _sub(x, j):
    return jnp.broadcast_to(x[j:j + 1, :], x.shape)

def sweep(C, sub):
    C = list(C)
    Wt = [jnp.zeros((8, 128), F32) for _ in range(8)]
    piv = jnp.ones((8, 128), F32)
    for j in range(0, 8, 2):
        a, b, c = _sub(C[j], j), _sub(C[j], j + 1), _sub(C[j + 1], j + 1)
        r = 1.0 / (a * c - b * b)
        i11, i12, i22 = c * r, -b * r, a * r
        ra = 1.0 / a
        e = b * ra
        piv = jnp.where(sub == j, a, jnp.where(sub == j + 1, c - b * e, piv))
        for k in range(j):
            low = C[k] - e * _sub(C[k], j)
            Wt[k] = jnp.where(sub == j, C[k], jnp.where(sub == j + 1, low, Wt[k]))
        Wt[j] = jnp.where(sub == j, 1.0, jnp.where(sub == j + 1, -e, Wt[j]))
        Wt[j + 1] = jnp.where(sub == j + 1, 1.0, Wt[j + 1])
        for k in range(8):
            if k not in (j, j + 1):
                q0, q1 = _sub(C[k], j), _sub(C[k], j + 1)
                s0 = i11 * q0 + i12 * q1
                s1 = i12 * q0 + i22 * q1
                new = C[k] - (C[j] * s0 + C[j + 1] * s1)
                C[k] = jnp.where(sub == j, s0, jnp.where(sub == j + 1, s1, new))
        x, y = C[j], C[j + 1]
        C[j] = jnp.where(sub == j, i11, jnp.where(sub == j + 1, i12, -(x * i11 + y * i12)))
        C[j + 1] = jnp.where(sub == j, i12, jnp.where(sub == j + 1, i22, -(x * i12 + y * i22)))
    rs = lax.rsqrt(piv)
    return C, [w * rs for w in Wt]

def tree(xs):
    xs = list(xs)
    while len(xs) > 1:
        xs = [xs[i] + xs[i + 1] if i + 1 < len(xs) else xs[i] for i in range(0, len(xs), 2)]
    return xs[0]

def invchol128(M, hook):
    n = len(M)
    M = list(M)
    sub = lax.broadcasted_iota(jnp.int32, (8, 128), 0)
    lane = lax.broadcasted_iota(jnp.int32, (8, 128), 1)
    out = []
    for k in range(n):
        hook(k)
        blk = (lane >= 8 * k) & (lane < 8 * k + 8)
        Cb = [[jnp.broadcast_to(M[i][:, 8 * k + u:8 * k + u + 1], (8, 128)) for u in range(8)]
              for i in range(k, min(k + 2, n))]
        m = jnp.where(blk, jnp.where(lane == 8 * k + sub, 1.0, 0.0), M[k])
        mb = [_sub(m, u) for u in range(8)]
        P, W8 = sweep([jnp.where(lane < 128, v, 0.0) for v in Cb[0]], sub)
        T = tree([P[u] * mb[u] for u in range(8)])
        Tb = [_sub(T, u) for u in range(8)]
        if k + 1 < n:
            M[k + 1] = jnp.where(blk, 0.0, M[k + 1]) - tree([Cb[1][u] * Tb[u] for u in range(8)])
        if k + 2 < n:
            update = dot(jnp.concatenate(M[k + 2:], axis=0)[:, 8 * k:8 * k + 8], T)
            for i in range(k + 2, n):
                M[i] = jnp.where(blk, 0.0, M[i]) - update[8 * (i - k - 2):8 * (i - k - 1)]
        row = tree([W8[u] * mb[u] for u in range(8)])
        out.append(jnp.where(lane < 8 * k + 8, row, 0.0))
    return out

def dot(a, b, dims=((1,), (0,))):
    return lax.dot_general(a, b, (dims, ((), ())), precision=HI, preferred_element_type=F32)

def rows_of(tiles, part):
    return jnp.concatenate([tiles[i, part] for i in range(16)], axis=0)


def inverse_factor(tiles, w, tmp, hook):
    o = invchol128([tiles[i, 0] for i in range(16)], lambda k: hook(0, k))
    for i in range(16):
        w[8 * i:8 * i + 8, 0:128] = o[i]
        w[8 * i:8 * i + 8, 128:256] = jnp.zeros((8, 128), F32)
    w11 = w[0:128, 0:128]
    l21 = dot(rows_of(tiles, 1), w11, ((1,), (1,)))
    s = rows_of(tiles, 2) - dot(l21, l21, ((1,), (1,)))
    tmp[...] = dot(l21, w11)
    o = invchol128([s[8 * i:8 * i + 8] for i in range(16)], lambda k: hook(1, k))
    for i in range(16):
        w[128 + 8 * i:136 + 8 * i, 128:256] = o[i]
    w[128:256, 0:128] = -dot(w[128:256, 128:256], tmp[...])


MESH = pl.DeviceIdType.MESH
NZ, NX, NY = 8, 4, 4
PLANE = NX * NY * 2
CUTS = (0, 1536, 3072, 4352, 5120)
CHUNKS = len(CUTS) - 1


def _wait(view, sem):
    pltpu.make_async_copy(view, view, sem).wait()


def _column(rows):
    r = rows.shape[0]
    return jnp.concatenate([rows, jnp.zeros((128 - r, 128), F32)], axis=0).T


class Ring4:
    def __init__(self, block, i, ids, plus, minus, sems, out):
        self.block, self.plus, self.minus, self.sems, self.out = block, plus, minus, sems, out
        self.i, self.ids = i, ids
        self.up, self.down, self.far = lax.rem(i + 1, 4), lax.rem(i + 3, 4), lax.rem(i + 2, 4)

    def send(self, q, owner, forward, slot):
        buf = self.plus if forward else self.minus
        pltpu.make_async_remote_copy(
            src_ref=self.block(q, owner),
            dst_ref=buf.at[slot],
            send_sem=self.sems.at[6 if forward else 7],
            recv_sem=self.sems.at[slot if forward else 3 + slot],
            device_id=self.ids(self.up if forward else self.down),
            device_id_type=MESH,
        ).start()

    def start(self):
        self.send(0, self.far, True, 0)
        self.send(1, self.far, False, 0)

    def middle(self):
        _wait(self.plus.at[0], self.sems.at[0])
        ref = self.block(0, self.up)
        ref[...] = ref[...] + self.plus[0]
        self.send(0, self.up, True, 2)
        _wait(self.minus.at[0], self.sems.at[3])
        ref = self.block(1, self.down)
        ref[...] = ref[...] + self.minus[0]
        self.send(1, self.down, False, 2)
        self.send(1, self.up, True, 1)
        self.send(0, self.down, False, 1)

    def finish(self):
        for s in (1, 2):
            _wait(self.plus.at[s], self.sems.at[s])
            _wait(self.minus.at[s], self.sems.at[3 + s])
        self.out[0] = self.block(0, self.i)[...] + (self.plus[2] + self.minus[1])
        self.out[1] = self.block(1, self.i)[...] + (self.plus[1] + self.minus[2])

    def drain(self):
        _wait(self.plus, self.sems.at[6])
        _wait(self.minus, self.sems.at[7])


class Ring8:
    def __init__(self, data, z, ids, plus, minus, sems):
        self.data, self.z, self.plus, self.minus, self.sems = data, z, plus, minus, sems
        self.next, self.last = ids(lax.rem(z + 1, 8)), ids(lax.rem(z + 7, 8))

    def send(self, step, src_up, src_down):
        lo, hi = (0, 2) if step == 0 else (4 * step - 2, 4 * step + 2)
        for src, buf, device, side in ((src_up, self.plus, self.next, 0), (src_down, self.minus, self.last, 1)):
            pltpu.make_async_remote_copy(
                src_ref=src, dst_ref=buf.at[lo:hi], send_sem=self.sems.at[8 + side],
                recv_sem=self.sems.at[4 * side + step], device_id=device, device_id_type=MESH).start()

    def start(self):
        far = lax.rem(self.z + 4, 8)
        self.send(0, self.data.at[far, 0:2], self.data.at[far, 2:4])

    def step(self, k):
        lo, hi = (0, 2) if k == 1 else (4 * k - 6, 4 * k - 2)
        up, down = lax.rem(self.z + 4 - k, 8), lax.rem(self.z + 4 + k, 8)
        for buf, at, part, side in ((self.plus, up, slice(0, 2), 0), (self.minus, down, slice(2, 4), 1)):
            _wait(buf.at[lo:hi], self.sems.at[4 * side + k - 1])
            ref = self.data.at[at, part] if k == 1 else self.data.at[at]
            ref[...] = ref[...] + buf[lo:hi]
        self.send(k, self.data.at[up], self.data.at[down])

    def finish(self, out):
        for side, buf in enumerate((self.plus, self.minus)):
            _wait(buf.at[10:14], self.sems.at[4 * side + 3])
        out[...] = self.data[self.z] + (self.plus[10:14] + self.minus[10:14])

    def drain(self):
        _wait(self.plus, self.sems.at[8])
        _wait(self.minus, self.sems.at[9])


def kernel(cells_all, counts, basis, scale, cells, cell_basis, gene_side,
           cbuf, bbuf, sbc, sk, wt, gl, gr, gp, zr, gz, gfull, w, tmp, stg, S, R, SZ, RZ, ZP, ZM, zt, zq,
           XP, XM, YP, YM, PX, PY, X2P, X2M, Y2P, Y2M, Q, zs, z3,
           load_sem, gsem, csem, rsem, zsem, qsem):
    sec = lax.axis_index("section")
    y = lax.axis_index("atlas")
    c = lax.rem(sec, 2)
    x = lax.rem(sec // 2, NX)
    z = sec // (2 * NX)
    h = x * NY + y

    def z_id(k):
        return ((k * NX + x) * 2 + c, y)

    def x_id(k):
        return ((z * NX + k) * 2 + c, y)

    def y_id(k):
        return (sec, k)

    partner = (sec + 1 - 2 * c, y)
    others = []
    for dx in (2, 1, 3, 0):
        for dy in (2, 1, 3, 0):
            if dx or dy:
                px, py = lax.rem(x + dx, NX), lax.rem(y + dy, NY)
                others.append((dx * NY + dy, px * NY + py, [((z * NX + px) * 2 + b, py) for b in range(2)]))

    def put(src, dst, pair, device):
        pltpu.make_async_remote_copy(
            src_ref=src, dst_ref=dst, send_sem=pair.at[0], recv_sem=pair.at[1],
            device_id=device, device_id_type=MESH).start()

    def by_core(fn):
        for b in range(2):
            pl.when(c == b)(functools.partial(fn, b))

    def alone(fn):
        pl.when(sec >= 0)(fn)

    def loads(k):
        cols = slice(CUTS[k], CUTS[k + 1])
        return (pltpu.make_async_copy(counts.at[:, cols], cbuf.at[:, cols], load_sem.at[0, k]),
                pltpu.make_async_copy(basis.at[cols, :], bbuf.at[cols, :], load_sem.at[1, k]))

    @alone
    def _():
        for k in range(CHUNKS):
            for copy in loads(k):
                copy.start()

    barrier = pltpu.get_barrier_semaphore()
    for _, _, ids in others:
        for device in ids:
            pl.semaphore_signal(barrier, inc=1, device_id=device, device_id_type=MESH)
    pl.semaphore_signal(barrier, inc=1, device_id=partner, device_id_type=MESH)

    @pl.loop(1, NZ)
    def _(d):
        pl.semaphore_signal(barrier, inc=1, device_id=z_id(lax.rem(z + d, NZ)), device_id_type=MESH)

    turned = _column(scale[...])
    for g in range(scale.shape[0]):
        sbc[128 * g:128 * g + 128, :] = jnp.broadcast_to(turned[:, g:g + 1], (128, 128))
    for k in range(CHUNKS):
        for copy in loads(k):
            copy.wait()
        rows = slice(CUTS[k], CUTS[k + 1])
        factor = sbc[rows, :]
        part = bbuf[rows, :].astype(F32)
        scaled = jnp.concatenate([part[:, :128] * factor, part[:, 128:] * factor], axis=1).astype(jnp.bfloat16)
        term = jnp.dot(cbuf[:, rows], scaled, preferred_element_type=F32)
        sk[...] = term if k == 0 else sk[...] + term

    turned = _column(cells[...])
    for r in range(cells.shape[0]):
        rows = slice(128 * r, 128 * r + 128)
        factor = jnp.broadcast_to(turned[:, r:r + 1], (128, 256))
        value = sk[rows, :] * factor
        sk[rows, :] = value
        wt[rows, :] = (value * factor).astype(jnp.bfloat16)

    gram = dot(sk[...], sk[...], ((0,), (0,))) * (1.0 / cells_all)
    for i in range(16):
        gl[i, 0] = gram[8 * i:8 * i + 8, :128]
        gl[i, 1] = gram[128 + 8 * i:136 + 8 * i, :128]
        gl[i, 2] = gram[128 + 8 * i:136 + 8 * i, 128:]

    pl.semaphore_wait(barrier, PLANE - 1 + NZ - 1)

    for r, chip, ids in others:
        place = (2 * r + c) * 2
        put(gl.at[chip, 0:1], gr.at[pl.ds(place, 1)], gsem.at[0], ids[0])
        put(gl.at[chip, 1:3], gr.at[pl.ds(place, 2)], gsem.at[0], ids[1])

    def to_partner(b):
        n = 2 - b
        put(gl.at[h, 1 - b:1 - b + n], gr.at[2 * b:2 * b + n], gsem.at[0], partner)
        gr[2 * b] = gl[h, b]
        gr[2 * b + 1] = gl[h, 2 * b]

    by_core(to_partner)

    def sums(batch, begin, end):
        @pl.loop(begin, end)
        def _(j):
            cols = pl.ds(pl.multiple_of((4 * batch + j) * 640, 128), 640)
            part = lax.dot_general(cbuf[:, cols], wt[...], (((0,), (0,)), ((), ())), preferred_element_type=F32)
            factor = sbc[cols, :] * (1.0 / cells_all)
            stg[:, :128] = part[:, :128] * factor
            stg[:, 128:] = part[:, 128:] * factor
            for a in range(NX):
                for b in range(2):
                    for e in range(NY):
                        o = ((a * 2 + b) * NY + e) * 20
                        S[b, batch, 0, j, a, e] = stg[o:o + 8, :128]
                        S[b, batch, 1, j, a, e] = stg[o:o + 8, 128:]
                        S[b, batch, 2, j, a, e] = stg[o + 8:o + 16, :128]
                        S[b, batch, 3, j, a, e] = stg[o + 8:o + 16, 128:]
                        SZ[b, 4 * batch + j, a, e] = jnp.concatenate(
                            [stg[o + 16:o + 20, :128], stg[o + 16:o + 20, 128:]], axis=0)
            put(S.at[1 - c, batch, :, j], R.at[batch, :, j], csem.at[batch], partner)
            put(SZ.at[1 - c, 4 * batch + j], RZ.at[4 * batch + j], csem.at[2], partner)

    sums(0, 0, 4)
    sums(1, 0, 2)

    first, second, third, fourth = [], [], [], []
    for batch in range(2):
        first.append(Ring4(lambda q, o, n=batch: R.at[n, q, :, o], x, x_id,
                           XP.at[batch], XM.at[batch], rsem.at[batch, 0], PX.at[batch]))
        second.append(Ring4(lambda q, o, n=batch: R.at[n, 2 + q, :, :, o], y, y_id,
                            YP.at[batch], YM.at[batch], rsem.at[batch, 1], PY.at[batch]))
        third.append(Ring4(lambda q, o, n=batch: PX.at[n, q, :, o], y, y_id,
                           X2P.at[batch], X2M.at[batch], rsem.at[batch, 2], Q.at[batch, 0:2]))
        fourth.append(Ring4(lambda q, o, n=batch: PY.at[n, q, :, o], x, x_id,
                            Y2P.at[batch], Y2M.at[batch], rsem.at[batch, 3], Q.at[batch, 2:4]))

    def add_partner(batch):
        _wait(R.at[batch], csem.at[batch, 1])

        @pl.loop(0, 4)
        def _(u):
            for q in range(4):
                R[batch, q, u] = R[batch, q, u] + S[c, batch, q, u]

    def stage_one(batch):
        first[batch].start()
        second[batch].start()

    def stage_one_middle(batch):
        first[batch].middle()
        second[batch].middle()

    def stage_two(batch):
        first[batch].finish()
        third[batch].start()
        second[batch].finish()
        fourth[batch].start()

    def stage_two_middle(batch):
        third[batch].middle()
        fourth[batch].middle()

    def stage_three(batch):
        third[batch].finish()
        fourth[batch].finish()
        for j in range(NZ // 2):
            k = 4 * batch + j
            for t in range(4):
                zs[k, t] = Q[batch, t, j]
            d = lax.rem(k - z + NZ, NZ)

            @pl.when(d > 0)
            def _():
                put(zs.at[k], z3.at[d - 1], zsem, z_id(k))

    over = Ring8(RZ, z, z_id, ZP, ZM, qsem)

    def z_start():
        _wait(RZ, csem.at[2, 1])

        @pl.loop(0, NZ)
        def _(k):
            RZ[k] = RZ[k] + SZ[c, k]

        over.start()

    def z_finish():
        over.finish(zt)
        zq[0] = zt[x, y]
        for r, chip, ids in others:
            pltpu.make_async_remote_copy(
                src_ref=zt.at[chip // NY, lax.rem(chip, NY)], dst_ref=zq.at[r], send_sem=qsem.at[10], recv_sem=qsem.at[11],
                device_id=(ids[0][0] + c, ids[0][1]), device_id_type=MESH).start()

    add_partner(0)
    alone(lambda: stage_one(0))
    sums(1, 2, 4)

    by_core(lambda b: _wait(gr.at[0:31 * (b + 1)], gsem.at[0, 1]))
    gp[...] = jnp.sum(gr[...].reshape(PLANE, 2, 8, 128), axis=0)

    def over_z(b):
        @pl.loop(1, NZ)
        def _(d):
            put(gp.at[0:b + 1], zr.at[pl.ds(2 * (d - 1), b + 1)], gsem.at[1], z_id(lax.rem(z + d, NZ)))

    by_core(over_z)

    add_partner(1)
    alone(z_start)
    alone(lambda: stage_one(1))

    alone(lambda: stage_one_middle(0))
    alone(lambda: over.step(1))

    by_core(lambda b: _wait(zr.at[0:7 * (b + 1)], gsem.at[1, 1]))
    gz[...] = gp[...] + jnp.sum(zr[...].reshape(NZ - 1, 2, 8, 128), axis=0)

    def spread(b):
        n = b + 1
        gfull[h, b] = gz[0]
        if b:
            gfull[h, 2] = gz[1]
        for _, _, ids in others:
            put(gz.at[0:n], gfull.at[h, b:b + n], gsem.at[2], ids[b])

    by_core(spread)

    alone(lambda: stage_one_middle(1))
    alone(lambda: over.step(2))
    alone(lambda: stage_two(0))

    def hand_over(b):
        n = b + 1
        _wait(gr.at[0:15 * n], gsem.at[2, 1])
        put(gfull.at[:, b:b + n], gfull.at[:, b:b + n], gsem.at[3], partner)

    by_core(hand_over)
    by_core(lambda b: _wait(gr.at[0:16 * (2 - b)], gsem.at[3, 1]))

    events = {
        (0, 4): lambda: stage_two(1),
        (0, 6): lambda: stage_two_middle(0),
        (0, 7): lambda: over.step(3),
        (0, 14): lambda: stage_two_middle(1),
        (1, 1): lambda: stage_three(0),
        (1, 3): z_finish,
        (1, 6): lambda: stage_three(1),
    }

    def hook(half, k):
        if (half, k) in events:
            with jax.named_scope(f"e{half}_{k}"):
                alone(events[half, k])

    inverse_factor(gfull, w, tmp, hook)

    cell_basis[...] = dot(sk[...], w[...], ((1,), (1,))).astype(jnp.bfloat16)

    _wait(z3, zsem.at[1])
    _wait(zq.at[1:16], qsem.at[11])
    own = zs[z] + jnp.sum(z3[...], axis=0)
    top = jnp.concatenate([own[0], own[1]], axis=1)
    mid = jnp.concatenate([own[2], own[3]], axis=1)
    rest = jnp.sum(zq[...], axis=0)
    low = jnp.concatenate([rest, pltpu.roll(rest, 4, 0)], axis=1)
    side = dot(jnp.concatenate([top, mid, low], axis=0), w[...], ((1,), (1,)))
    gene_side[...] = side[:20]

    def drain(b):
        _wait(gr.at[0:47 - b], gsem.at[0, 0])
        _wait(zr.at[0:7 * (b + 1)], gsem.at[1, 0])
        _wait(gr.at[0:15 * (b + 1)], gsem.at[2, 0])
        _wait(gr.at[0:16 * (b + 1)], gsem.at[3, 0])

    by_core(drain)
    for batch in range(2):
        _wait(R.at[batch], csem.at[batch, 0])
        for ring in (first[batch], second[batch], third[batch], fourth[batch]):
            ring.drain()
    _wait(z3, zsem.at[0])
    _wait(RZ, csem.at[2, 0])
    over.drain()
    _wait(zq.at[1:16], qsem.at[10])


def hand_on(a, b, a_out, b_out):
    a_out[...] = a[...]
    b_out[...] = b[...]


def local(counts, gene_scale, cell_scale, gene_basis):
    device_count = lax.axis_size("section") * lax.axis_size("atlas")
    rows, genes = counts.shape
    vm = lambda *s: pltpu.VMEM(s, F32)
    dma = pltpu.SemaphoreType.DMA
    shapes = (jax.ShapeDtypeStruct((rows, 256), jnp.bfloat16),
              jax.ShapeDtypeStruct((genes // device_count, 256), F32))
    result = pl.pallas_call(
        functools.partial(kernel, rows * device_count),
        out_shape=shapes,
        in_specs=[pl.BlockSpec(memory_space=pl.ANY)] * 2 + [pl.BlockSpec(memory_space=pltpu.VMEM)] * 2,
        out_specs=(pl.BlockSpec(memory_space=pltpu.VMEM),) * 2,
        scratch_shapes=[
            pltpu.VMEM((rows, genes), jnp.bfloat16), pltpu.VMEM((genes, 256), jnp.bfloat16),
            vm(genes, 128), vm(rows, 256), pltpu.VMEM((rows, 256), jnp.bfloat16),
            vm(16, 3, 8, 128), vm(64, 8, 128), vm(2, 8, 128), vm(14, 8, 128), vm(2, 8, 128),
            vm(16, 3, 8, 128), vm(256, 256), vm(128, 128), vm(640, 256),
            vm(2, 2, 4, 4, NX, NY, 8, 128), vm(2, 4, 4, NX, NY, 8, 128),
            vm(2, NZ, NX, NY, 8, 128), vm(NZ, NX, NY, 8, 128), vm(14, NY, 8, 128), vm(14, NY, 8, 128),
            vm(NX, NY, 8, 128), vm(NX * NY, 8, 128),
            vm(2, 3, 4, 4, 8, 128), vm(2, 3, 4, 4, 8, 128), vm(2, 3, 4, 4, 8, 128), vm(2, 3, 4, 4, 8, 128),
            vm(2, 2, 4, 4, 8, 128), vm(2, 2, 4, 4, 8, 128),
            vm(2, 3, 4, 8, 128), vm(2, 3, 4, 8, 128), vm(2, 3, 4, 8, 128), vm(2, 3, 4, 8, 128),
            vm(2, 4, 4, 8, 128), vm(NZ, 4, 8, 128), vm(NZ - 1, 4, 8, 128),
            dma((2, CHUNKS)), dma((4, 2)), dma((3, 2)), dma((2, 4, 8)), dma((2,)), dma((12,)),
        ],
        compiler_params=pltpu.CompilerParams(collective_id=0, has_side_effects=True, vmem_limit_bytes=60 << 20),
    )(counts, gene_basis, gene_scale.reshape(genes // 128, 128), cell_scale.reshape(rows // 128, 128))
    return pl.pallas_call(hand_on, out_shape=shapes)(*result)


def solution(mesh):
    return jax.shard_map(
        local,
        mesh=mesh,
        in_specs=(P(("section", "atlas"), None), P(), P(("section", "atlas")), P()),
        out_specs=(P(("section", "atlas"), None), P(("section", "atlas"), None)),
        check_vma=False,
    )
```

```python
import functools

import jax
import jax.numpy as jnp
from jax import lax
from jax.experimental import pallas as pl
from jax.experimental.pallas import tpu as pltpu
from jax.sharding import PartitionSpec as P

HI = lax.Precision.HIGHEST
F32 = jnp.float32

def _sub(x, j):
    return jnp.broadcast_to(x[j:j + 1, :], x.shape)

def sweep(C, sub):
    C = list(C)
    Wt = [jnp.zeros((8, 128), F32) for _ in range(8)]
    piv = jnp.ones((8, 128), F32)
    for j in range(0, 8, 2):
        a, b, c = _sub(C[j], j), _sub(C[j], j + 1), _sub(C[j + 1], j + 1)
        r = 1.0 / (a * c - b * b)
        i11, i12, i22 = c * r, -b * r, a * r
        ra = 1.0 / a
        e = b * ra
        piv = jnp.where(sub == j, a, jnp.where(sub == j + 1, c - b * e, piv))
        for k in range(j):
            low = C[k] - e * _sub(C[k], j)
            Wt[k] = jnp.where(sub == j, C[k], jnp.where(sub == j + 1, low, Wt[k]))
        Wt[j] = jnp.where(sub == j, 1.0, jnp.where(sub == j + 1, -e, Wt[j]))
        Wt[j + 1] = jnp.where(sub == j + 1, 1.0, Wt[j + 1])
        for k in range(8):
            if k not in (j, j + 1):
                q0, q1 = _sub(C[k], j), _sub(C[k], j + 1)
                s0 = i11 * q0 + i12 * q1
                s1 = i12 * q0 + i22 * q1
                new = C[k] - (C[j] * s0 + C[j + 1] * s1)
                C[k] = jnp.where(sub == j, s0, jnp.where(sub == j + 1, s1, new))
        x, y = C[j], C[j + 1]
        C[j] = jnp.where(sub == j, i11, jnp.where(sub == j + 1, i12, -(x * i11 + y * i12)))
        C[j + 1] = jnp.where(sub == j, i12, jnp.where(sub == j + 1, i22, -(x * i12 + y * i22)))
    rs = lax.rsqrt(piv)
    return C, [w * rs for w in Wt]

def tree(xs):
    xs = list(xs)
    while len(xs) > 1:
        xs = [xs[i] + xs[i + 1] if i + 1 < len(xs) else xs[i] for i in range(0, len(xs), 2)]
    return xs[0]

def invchol128(M, hook):
    n = len(M)
    M = list(M)
    sub = lax.broadcasted_iota(jnp.int32, (8, 128), 0)
    lane = lax.broadcasted_iota(jnp.int32, (8, 128), 1)
    out = []
    for k in range(n):
        hook(k)
        blk = (lane >= 8 * k) & (lane < 8 * k + 8)
        Cb = [[jnp.broadcast_to(M[i][:, 8 * k + u:8 * k + u + 1], (8, 128)) for u in range(8)]
              for i in range(k, min(k + 2, n))]
        m = jnp.where(blk, jnp.where(lane == 8 * k + sub, 1.0, 0.0), M[k])
        mb = [_sub(m, u) for u in range(8)]
        P, W8 = sweep([jnp.where(lane < 128, v, 0.0) for v in Cb[0]], sub)
        T = tree([P[u] * mb[u] for u in range(8)])
        Tb = [_sub(T, u) for u in range(8)]
        if k + 1 < n:
            M[k + 1] = jnp.where(blk, 0.0, M[k + 1]) - tree([Cb[1][u] * Tb[u] for u in range(8)])
        if k + 2 < n:
            update = dot(jnp.concatenate(M[k + 2:], axis=0)[:, 8 * k:8 * k + 8], T)
            for i in range(k + 2, n):
                M[i] = jnp.where(blk, 0.0, M[i]) - update[8 * (i - k - 2):8 * (i - k - 1)]
        row = tree([W8[u] * mb[u] for u in range(8)])
        out.append(jnp.where(lane < 8 * k + 8, row, 0.0))
    return out

def dot(a, b, dims=((1,), (0,))):
    return lax.dot_general(a, b, (dims, ((), ())), precision=HI, preferred_element_type=F32)

def rows_of(tiles, part):
    return jnp.concatenate([tiles[i, part] for i in range(16)], axis=0)


def inverse_factor(tiles, w, tmp, hook):
    o = invchol128([tiles[i, 0] for i in range(16)], lambda k: hook(0, k))
    for i in range(16):
        w[8 * i:8 * i + 8, 0:128] = o[i]
        w[8 * i:8 * i + 8, 128:256] = jnp.zeros((8, 128), F32)
    w11 = w[0:128, 0:128]
    l21 = dot(rows_of(tiles, 1), w11, ((1,), (1,)))
    s = rows_of(tiles, 2) - dot(l21, l21, ((1,), (1,)))
    tmp[...] = dot(l21, w11)
    o = invchol128([s[8 * i:8 * i + 8] for i in range(16)], lambda k: hook(1, k))
    for i in range(16):
        w[128 + 8 * i:136 + 8 * i, 128:256] = o[i]
    w[128:256, 0:128] = -dot(w[128:256, 128:256], tmp[...])


MESH = pl.DeviceIdType.MESH
NZ, NX, NY = 8, 4, 4
PLANE = NX * NY * 2
CUTS = (0, 1536, 3072, 4352, 5120)
CHUNKS = len(CUTS) - 1


def _wait(view, sem):
    pltpu.make_async_copy(view, view, sem).wait()


def _column(rows):
    r = rows.shape[0]
    return jnp.concatenate([rows, jnp.zeros((128 - r, 128), F32)], axis=0).T


class Ring4:
    def __init__(self, block, i, ids, plus, minus, sems, out):
        self.block, self.plus, self.minus, self.sems, self.out = block, plus, minus, sems, out
        self.i, self.ids = i, ids
        self.up, self.down, self.far = lax.rem(i + 1, 4), lax.rem(i + 3, 4), lax.rem(i + 2, 4)

    def send(self, q, owner, forward, slot):
        buf = self.plus if forward else self.minus
        pltpu.make_async_remote_copy(
            src_ref=self.block(q, owner),
            dst_ref=buf.at[slot],
            send_sem=self.sems.at[6 if forward else 7],
            recv_sem=self.sems.at[slot if forward else 3 + slot],
            device_id=self.ids(self.up if forward else self.down),
            device_id_type=MESH,
        ).start()

    def start(self):
        self.send(0, self.far, True, 0)
        self.send(1, self.far, False, 0)

    def middle(self):
        _wait(self.plus.at[0], self.sems.at[0])
        ref = self.block(0, self.up)
        ref[...] = ref[...] + self.plus[0]
        self.send(0, self.up, True, 2)
        _wait(self.minus.at[0], self.sems.at[3])
        ref = self.block(1, self.down)
        ref[...] = ref[...] + self.minus[0]
        self.send(1, self.down, False, 2)
        self.send(1, self.up, True, 1)
        self.send(0, self.down, False, 1)

    def finish(self):
        for s in (1, 2):
            _wait(self.plus.at[s], self.sems.at[s])
            _wait(self.minus.at[s], self.sems.at[3 + s])
        self.out[0] = self.block(0, self.i)[...] + (self.plus[2] + self.minus[1])
        self.out[1] = self.block(1, self.i)[...] + (self.plus[1] + self.minus[2])

    def drain(self):
        _wait(self.plus, self.sems.at[6])
        _wait(self.minus, self.sems.at[7])


class Ring8:
    def __init__(self, data, z, ids, plus, minus, sems):
        self.data, self.z, self.plus, self.minus, self.sems = data, z, plus, minus, sems
        self.next, self.last = ids(lax.rem(z + 1, 8)), ids(lax.rem(z + 7, 8))

    def send(self, step, src_up, src_down):
        lo, hi = (0, 2) if step == 0 else (4 * step - 2, 4 * step + 2)
        for src, buf, device, side in ((src_up, self.plus, self.next, 0), (src_down, self.minus, self.last, 1)):
            pltpu.make_async_remote_copy(
                src_ref=src, dst_ref=buf.at[lo:hi], send_sem=self.sems.at[8 + side],
                recv_sem=self.sems.at[4 * side + step], device_id=device, device_id_type=MESH).start()

    def start(self):
        far = lax.rem(self.z + 4, 8)
        self.send(0, self.data.at[far, 0:2], self.data.at[far, 2:4])

    def step(self, k):
        lo, hi = (0, 2) if k == 1 else (4 * k - 6, 4 * k - 2)
        up, down = lax.rem(self.z + 4 - k, 8), lax.rem(self.z + 4 + k, 8)
        for buf, at, part, side in ((self.plus, up, slice(0, 2), 0), (self.minus, down, slice(2, 4), 1)):
            _wait(buf.at[lo:hi], self.sems.at[4 * side + k - 1])
            ref = self.data.at[at, part] if k == 1 else self.data.at[at]
            ref[...] = ref[...] + buf[lo:hi]
        self.send(k, self.data.at[up], self.data.at[down])

    def finish(self, out):
        for side, buf in enumerate((self.plus, self.minus)):
            _wait(buf.at[10:14], self.sems.at[4 * side + 3])
        out[...] = self.data[self.z] + (self.plus[10:14] + self.minus[10:14])

    def drain(self):
        _wait(self.plus, self.sems.at[8])
        _wait(self.minus, self.sems.at[9])


def kernel(cells_all, counts, basis, scale, cells, cell_basis, gene_side,
           cbuf, bbuf, sbc, sk, wt, gl, gr, gp, zr, gz, gfull, w, tmp, stg, S, R, SZ, RZ, ZP, ZM, zt, zq,
           XP, XM, YP, YM, PX, PY, X2P, X2M, Y2P, Y2M, Q, zs, z3,
           high, low_part, load_sem, gsem, csem, rsem, zsem, qsem):
    sec = lax.axis_index("section")
    y = lax.axis_index("atlas")
    c = lax.rem(sec, 2)
    x = lax.rem(sec // 2, NX)
    z = sec // (2 * NX)
    h = x * NY + y

    def z_id(k):
        return ((k * NX + x) * 2 + c, y)

    def x_id(k):
        return ((z * NX + k) * 2 + c, y)

    def y_id(k):
        return (sec, k)

    partner = (sec + 1 - 2 * c, y)
    others = []
    for dx in (2, 1, 3, 0):
        for dy in (2, 1, 3, 0):
            if dx or dy:
                px, py = lax.rem(x + dx, NX), lax.rem(y + dy, NY)
                others.append((dx * NY + dy, px * NY + py, [((z * NX + px) * 2 + b, py) for b in range(2)]))

    def put(src, dst, pair, device):
        pltpu.make_async_remote_copy(
            src_ref=src, dst_ref=dst, send_sem=pair.at[0], recv_sem=pair.at[1],
            device_id=device, device_id_type=MESH).start()

    def by_core(fn):
        for b in range(2):
            pl.when(c == b)(functools.partial(fn, b))

    def alone(fn):
        pl.when(sec >= 0)(fn)

    def loads(k):
        cols = slice(CUTS[k], CUTS[k + 1])
        return (pltpu.make_async_copy(counts.at[:, cols], cbuf.at[:, cols], load_sem.at[0, k]),
                pltpu.make_async_copy(basis.at[cols, :], bbuf.at[cols, :], load_sem.at[1, k]))

    @alone
    def _():
        for k in range(CHUNKS):
            for copy in loads(k):
                copy.start()

    barrier = pltpu.get_barrier_semaphore()
    for _, _, ids in others:
        for device in ids:
            pl.semaphore_signal(barrier, inc=1, device_id=device, device_id_type=MESH)
    pl.semaphore_signal(barrier, inc=1, device_id=partner, device_id_type=MESH)

    @pl.loop(1, NZ)
    def _(d):
        pl.semaphore_signal(barrier, inc=1, device_id=z_id(lax.rem(z + d, NZ)), device_id_type=MESH)

    turned = _column(scale[...])
    for g in range(scale.shape[0]):
        sbc[128 * g:128 * g + 128, :] = jnp.broadcast_to(turned[:, g:g + 1], (128, 128))
    for k in range(CHUNKS):
        for copy in loads(k):
            copy.wait()
        rows = slice(CUTS[k], CUTS[k + 1])
        factor = sbc[rows, :]
        part = bbuf[rows, :].astype(F32)
        scaled = jnp.concatenate([part[:, :128] * factor, part[:, 128:] * factor], axis=1).astype(jnp.bfloat16)
        term = jnp.dot(cbuf[:, rows], scaled, preferred_element_type=F32)
        sk[...] = term if k == 0 else sk[...] + term

    turned = _column(cells[...])
    for r in range(cells.shape[0]):
        rows = slice(128 * r, 128 * r + 128)
        factor = jnp.broadcast_to(turned[:, r:r + 1], (128, 256))
        value = sk[rows, :] * factor
        sk[rows, :] = value
        wt[rows, :] = (value * factor).astype(jnp.bfloat16)

    gram = dot(sk[...], sk[...], ((0,), (0,))) * (1.0 / cells_all)
    for i in range(16):
        gl[i, 0] = gram[8 * i:8 * i + 8, :128]
        gl[i, 1] = gram[128 + 8 * i:136 + 8 * i, :128]
        gl[i, 2] = gram[128 + 8 * i:136 + 8 * i, 128:]

    pl.semaphore_wait(barrier, PLANE - 1 + NZ - 1)

    for r, chip, ids in others:
        place = (2 * r + c) * 2
        put(gl.at[chip, 0:1], gr.at[pl.ds(place, 1)], gsem.at[0], ids[0])
        put(gl.at[chip, 1:3], gr.at[pl.ds(place, 2)], gsem.at[0], ids[1])

    def to_partner(b):
        n = 2 - b
        put(gl.at[h, 1 - b:1 - b + n], gr.at[2 * b:2 * b + n], gsem.at[0], partner)
        gr[2 * b] = gl[h, b]
        gr[2 * b + 1] = gl[h, 2 * b]

    by_core(to_partner)

    def sums(batch, begin, end):
        @pl.loop(begin, end)
        def _(j):
            cols = pl.ds(pl.multiple_of((4 * batch + j) * 640, 128), 640)
            part = lax.dot_general(cbuf[:, cols], wt[...], (((0,), (0,)), ((), ())), preferred_element_type=F32)
            factor = sbc[cols, :] * (1.0 / cells_all)
            stg[:, :128] = part[:, :128] * factor
            stg[:, 128:] = part[:, 128:] * factor
            for a in range(NX):
                for b in range(2):
                    for e in range(NY):
                        o = ((a * 2 + b) * NY + e) * 20
                        S[b, batch, 0, j, a, e] = stg[o:o + 8, :128]
                        S[b, batch, 1, j, a, e] = stg[o:o + 8, 128:]
                        S[b, batch, 2, j, a, e] = stg[o + 8:o + 16, :128]
                        S[b, batch, 3, j, a, e] = stg[o + 8:o + 16, 128:]
                        SZ[b, 4 * batch + j, a, e] = jnp.concatenate(
                            [stg[o + 16:o + 20, :128], stg[o + 16:o + 20, 128:]], axis=0)
            put(S.at[1 - c, batch, :, j], R.at[batch, :, j], csem.at[batch], partner)
            put(SZ.at[1 - c, 4 * batch + j], RZ.at[4 * batch + j], csem.at[2], partner)

    sums(0, 0, 4)
    sums(1, 0, 2)

    first, second, third, fourth = [], [], [], []
    for batch in range(2):
        first.append(Ring4(lambda q, o, n=batch: R.at[n, q, :, o], x, x_id,
                           XP.at[batch], XM.at[batch], rsem.at[batch, 0], PX.at[batch]))
        second.append(Ring4(lambda q, o, n=batch: R.at[n, 2 + q, :, :, o], y, y_id,
                            YP.at[batch], YM.at[batch], rsem.at[batch, 1], PY.at[batch]))
        third.append(Ring4(lambda q, o, n=batch: PX.at[n, q, :, o], y, y_id,
                           X2P.at[batch], X2M.at[batch], rsem.at[batch, 2], Q.at[batch, 0:2]))
        fourth.append(Ring4(lambda q, o, n=batch: PY.at[n, q, :, o], x, x_id,
                            Y2P.at[batch], Y2M.at[batch], rsem.at[batch, 3], Q.at[batch, 2:4]))

    def add_partner(batch):
        _wait(R.at[batch], csem.at[batch, 1])

        @pl.loop(0, 4)
        def _(u):
            for q in range(4):
                R[batch, q, u] = R[batch, q, u] + S[c, batch, q, u]

    def stage_one(batch):
        first[batch].start()
        second[batch].start()

    def stage_one_middle(batch):
        first[batch].middle()
        second[batch].middle()

    def stage_two(batch):
        first[batch].finish()
        third[batch].start()
        second[batch].finish()
        fourth[batch].start()

    def stage_two_middle(batch):
        third[batch].middle()
        fourth[batch].middle()

    def stage_three(batch):
        third[batch].finish()
        fourth[batch].finish()
        for j in range(NZ // 2):
            k = 4 * batch + j
            for t in range(4):
                zs[k, t] = Q[batch, t, j]
            d = lax.rem(k - z + NZ, NZ)

            @pl.when(d > 0)
            def _():
                put(zs.at[k], z3.at[d - 1], zsem, z_id(k))

    over = Ring8(RZ, z, z_id, ZP, ZM, qsem)

    def z_start():
        _wait(RZ, csem.at[2, 1])

        @pl.loop(0, NZ)
        def _(k):
            RZ[k] = RZ[k] + SZ[c, k]

        over.start()

    def z_finish():
        over.finish(zt)
        zq[0] = zt[x, y]
        for r, chip, ids in others:
            pltpu.make_async_remote_copy(
                src_ref=zt.at[chip // NY, lax.rem(chip, NY)], dst_ref=zq.at[r], send_sem=qsem.at[10], recv_sem=qsem.at[11],
                device_id=(ids[0][0] + c, ids[0][1]), device_id_type=MESH).start()

    add_partner(0)
    alone(lambda: stage_one(0))
    sums(1, 2, 4)

    by_core(lambda b: _wait(gr.at[0:31 * (b + 1)], gsem.at[0, 1]))
    gp[...] = jnp.sum(gr[...].reshape(PLANE, 2, 8, 128), axis=0)

    def over_z(b):
        @pl.loop(1, NZ)
        def _(d):
            put(gp.at[0:b + 1], zr.at[pl.ds(2 * (d - 1), b + 1)], gsem.at[1], z_id(lax.rem(z + d, NZ)))

    by_core(over_z)

    add_partner(1)
    alone(z_start)
    alone(lambda: stage_one(1))

    alone(lambda: stage_one_middle(0))
    alone(lambda: over.step(1))

    by_core(lambda b: _wait(zr.at[0:7 * (b + 1)], gsem.at[1, 1]))
    gz[...] = gp[...] + jnp.sum(zr[...].reshape(NZ - 1, 2, 8, 128), axis=0)

    def spread(b):
        n = b + 1
        gfull[h, b] = gz[0]
        if b:
            gfull[h, 2] = gz[1]
        for _, _, ids in others:
            put(gz.at[0:n], gfull.at[h, b:b + n], gsem.at[2], ids[b])

    by_core(spread)

    def split(value, at):
        top_part = value.astype(jnp.bfloat16)
        high[at, :] = top_part
        low_part[at, :] = (value - top_part.astype(F32)).astype(jnp.bfloat16)

    split(sk[...], slice(0, sk.shape[0]))
    alone(lambda: stage_one_middle(1))
    alone(lambda: over.step(2))
    alone(lambda: stage_two(0))

    def hand_over(b):
        n = b + 1
        _wait(gr.at[0:15 * n], gsem.at[2, 1])
        put(gfull.at[:, b:b + n], gfull.at[:, b:b + n], gsem.at[3], partner)

    by_core(hand_over)
    by_core(lambda b: _wait(gr.at[0:16 * (2 - b)], gsem.at[3, 1]))

    events = {
        (0, 4): lambda: stage_two(1),
        (0, 6): lambda: stage_two_middle(0),
        (0, 7): lambda: over.step(3),
        (0, 14): lambda: stage_two_middle(1),
        (1, 1): lambda: stage_three(0),
        (1, 3): z_finish,
        (1, 6): lambda: stage_three(1),
    }

    def hook(half, k):
        if (half, k) in events:
            with jax.named_scope(f"e{half}_{k}"):
                alone(events[half, k])

    inverse_factor(gfull, w, tmp, hook)

    _wait(z3, zsem.at[1])
    _wait(zq.at[1:16], qsem.at[11])
    own = zs[z] + jnp.sum(z3[...], axis=0)
    top = jnp.concatenate([own[0], own[1]], axis=1)
    mid = jnp.concatenate([own[2], own[3]], axis=1)
    rest = jnp.sum(zq[...], axis=0)
    low = jnp.concatenate([rest, pltpu.roll(rest, 4, 0)], axis=1)
    rows = sk.shape[0]
    split(jnp.concatenate([top, mid, low, jnp.zeros_like(low)], axis=0), slice(rows, rows + 32))
    factor = w[...]
    factor_high = factor.astype(jnp.bfloat16)
    factor_low = (factor - factor_high.astype(F32)).astype(jnp.bfloat16)

    def times(a, b):
        return lax.dot_general(a, b, (((1,), (1,)), ((), ())), preferred_element_type=F32)

    both = times(high[...], factor_high) + (times(high[...], factor_low) + times(low_part[...], factor_high))
    cell_basis[...] = both[:rows].astype(jnp.bfloat16)
    gene_side[...] = both[rows:rows + 20]

    def drain(b):
        _wait(gr.at[0:47 - b], gsem.at[0, 0])
        _wait(zr.at[0:7 * (b + 1)], gsem.at[1, 0])
        _wait(gr.at[0:15 * (b + 1)], gsem.at[2, 0])
        _wait(gr.at[0:16 * (b + 1)], gsem.at[3, 0])

    by_core(drain)
    for batch in range(2):
        _wait(R.at[batch], csem.at[batch, 0])
        for ring in (first[batch], second[batch], third[batch], fourth[batch]):
            ring.drain()
    _wait(z3, zsem.at[0])
    _wait(RZ, csem.at[2, 0])
    over.drain()
    _wait(zq.at[1:16], qsem.at[10])


def hand_on(a, b, a_out, b_out):
    a_out[...] = a[...]
    b_out[...] = b[...]


def local(counts, gene_scale, cell_scale, gene_basis):
    device_count = lax.axis_size("section") * lax.axis_size("atlas")
    rows, genes = counts.shape
    vm = lambda *s: pltpu.VMEM(s, F32)
    dma = pltpu.SemaphoreType.DMA
    shapes = (jax.ShapeDtypeStruct((rows, 256), jnp.bfloat16),
              jax.ShapeDtypeStruct((genes // device_count, 256), F32))
    result = pl.pallas_call(
        functools.partial(kernel, rows * device_count),
        out_shape=shapes,
        in_specs=[pl.BlockSpec(memory_space=pl.ANY)] * 2 + [pl.BlockSpec(memory_space=pltpu.VMEM)] * 2,
        out_specs=(pl.BlockSpec(memory_space=pltpu.VMEM),) * 2,
        scratch_shapes=[
            pltpu.VMEM((rows, genes), jnp.bfloat16), pltpu.VMEM((genes, 256), jnp.bfloat16),
            vm(genes, 128), vm(rows, 256), pltpu.VMEM((rows, 256), jnp.bfloat16),
            vm(16, 3, 8, 128), vm(64, 8, 128), vm(2, 8, 128), vm(14, 8, 128), vm(2, 8, 128),
            vm(16, 3, 8, 128), vm(256, 256), vm(128, 128), vm(640, 256),
            vm(2, 2, 4, 4, NX, NY, 8, 128), vm(2, 4, 4, NX, NY, 8, 128),
            vm(2, NZ, NX, NY, 8, 128), vm(NZ, NX, NY, 8, 128), vm(14, NY, 8, 128), vm(14, NY, 8, 128),
            vm(NX, NY, 8, 128), vm(NX * NY, 8, 128),
            vm(2, 3, 4, 4, 8, 128), vm(2, 3, 4, 4, 8, 128), vm(2, 3, 4, 4, 8, 128), vm(2, 3, 4, 4, 8, 128),
            vm(2, 2, 4, 4, 8, 128), vm(2, 2, 4, 4, 8, 128),
            vm(2, 3, 4, 8, 128), vm(2, 3, 4, 8, 128), vm(2, 3, 4, 8, 128), vm(2, 3, 4, 8, 128),
            vm(2, 4, 4, 8, 128), vm(NZ, 4, 8, 128), vm(NZ - 1, 4, 8, 128),
            pltpu.VMEM((rows + 32, 256), jnp.bfloat16), pltpu.VMEM((rows + 32, 256), jnp.bfloat16),
            dma((2, CHUNKS)), dma((4, 2)), dma((3, 2)), dma((2, 4, 8)), dma((2,)), dma((12,)),
        ],
        compiler_params=pltpu.CompilerParams(collective_id=0, has_side_effects=True, vmem_limit_bytes=60 << 20),
    )(counts, gene_basis, gene_scale.reshape(genes // 128, 128), cell_scale.reshape(rows // 128, 128))
    return pl.pallas_call(hand_on, out_shape=shapes)(*result)


def solution(mesh):
    return jax.shard_map(
        local,
        mesh=mesh,
        in_specs=(P(("section", "atlas"), None), P(), P(("section", "atlas")), P()),
        out_specs=(P(("section", "atlas"), None), P(("section", "atlas"), None)),
        check_vma=False,
    )
```

```python
import functools

import jax
import jax.numpy as jnp
from jax import lax
from jax.experimental import pallas as pl
from jax.experimental.pallas import tpu as pltpu
from jax.sharding import PartitionSpec as P

HI = lax.Precision.HIGHEST
F32 = jnp.float32

def _sub(x, j):
    return jnp.broadcast_to(x[j:j + 1, :], x.shape)

def sweep(C, sub):
    C = list(C)
    Wt = [jnp.zeros((8, 128), F32) for _ in range(8)]
    piv = jnp.ones((8, 128), F32)
    for j in range(0, 8, 2):
        a, b, c = _sub(C[j], j), _sub(C[j], j + 1), _sub(C[j + 1], j + 1)
        r = 1.0 / (a * c - b * b)
        i11, i12, i22 = c * r, -b * r, a * r
        ra = 1.0 / a
        e = b * ra
        piv = jnp.where(sub == j, a, jnp.where(sub == j + 1, c - b * e, piv))
        for k in range(j):
            low = C[k] - e * _sub(C[k], j)
            Wt[k] = jnp.where(sub == j, C[k], jnp.where(sub == j + 1, low, Wt[k]))
        Wt[j] = jnp.where(sub == j, 1.0, jnp.where(sub == j + 1, -e, Wt[j]))
        Wt[j + 1] = jnp.where(sub == j + 1, 1.0, Wt[j + 1])
        for k in range(8):
            if k not in (j, j + 1):
                q0, q1 = _sub(C[k], j), _sub(C[k], j + 1)
                s0 = i11 * q0 + i12 * q1
                s1 = i12 * q0 + i22 * q1
                new = C[k] - (C[j] * s0 + C[j + 1] * s1)
                C[k] = jnp.where(sub == j, s0, jnp.where(sub == j + 1, s1, new))
        x, y = C[j], C[j + 1]
        C[j] = jnp.where(sub == j, i11, jnp.where(sub == j + 1, i12, -(x * i11 + y * i12)))
        C[j + 1] = jnp.where(sub == j, i12, jnp.where(sub == j + 1, i22, -(x * i12 + y * i22)))
    rs = lax.rsqrt(piv)
    return C, [w * rs for w in Wt]

def tree(xs):
    xs = list(xs)
    while len(xs) > 1:
        xs = [xs[i] + xs[i + 1] if i + 1 < len(xs) else xs[i] for i in range(0, len(xs), 2)]
    return xs[0]

def invchol128(M, hook):
    n = len(M)
    M = list(M)
    sub = lax.broadcasted_iota(jnp.int32, (8, 128), 0)
    lane = lax.broadcasted_iota(jnp.int32, (8, 128), 1)
    out = []
    for k in range(n):
        hook(k)
        blk = (lane >= 8 * k) & (lane < 8 * k + 8)
        Cb = [[jnp.broadcast_to(M[i][:, 8 * k + u:8 * k + u + 1], (8, 128)) for u in range(8)]
              for i in range(k, min(k + 2, n))]
        m = jnp.where(blk, jnp.where(lane == 8 * k + sub, 1.0, 0.0), M[k])
        mb = [_sub(m, u) for u in range(8)]
        P, W8 = sweep([jnp.where(lane < 128, v, 0.0) for v in Cb[0]], sub)
        T = tree([P[u] * mb[u] for u in range(8)])
        Tb = [_sub(T, u) for u in range(8)]
        if k + 1 < n:
            M[k + 1] = jnp.where(blk, 0.0, M[k + 1]) - tree([Cb[1][u] * Tb[u] for u in range(8)])
        if k + 2 < n:
            update = dot(jnp.concatenate(M[k + 2:], axis=0)[:, 8 * k:8 * k + 8], T)
            for i in range(k + 2, n):
                M[i] = jnp.where(blk, 0.0, M[i]) - update[8 * (i - k - 2):8 * (i - k - 1)]
        row = tree([W8[u] * mb[u] for u in range(8)])
        out.append(jnp.where(lane < 8 * k + 8, row, 0.0))
    return out

def dot(a, b, dims=((1,), (0,))):
    return lax.dot_general(a, b, (dims, ((), ())), precision=HI, preferred_element_type=F32)

def rows_of(tiles, part):
    return jnp.concatenate([tiles[i, part] for i in range(16)], axis=0)


def inverse_factor(tiles, w, tmp, hook):
    o = invchol128([tiles[i, 0] for i in range(16)], lambda k: hook(0, k))
    for i in range(16):
        w[8 * i:8 * i + 8, 0:128] = o[i]
        w[8 * i:8 * i + 8, 128:256] = jnp.zeros((8, 128), F32)
    w11 = w[0:128, 0:128]
    l21 = dot(rows_of(tiles, 1), w11, ((1,), (1,)))
    s = rows_of(tiles, 2) - dot(l21, l21, ((1,), (1,)))
    tmp[...] = dot(l21, w11)
    o = invchol128([s[8 * i:8 * i + 8] for i in range(16)], lambda k: hook(1, k))
    for i in range(16):
        w[128 + 8 * i:136 + 8 * i, 128:256] = o[i]
    w[128:256, 0:128] = -dot(w[128:256, 128:256], tmp[...])


MESH = pl.DeviceIdType.MESH
NZ, NX, NY = 8, 4, 4
PLANE = NX * NY * 2
CUTS = (0, 1536, 3072, 4352, 5120)
CHUNKS = len(CUTS) - 1


def _wait(view, sem):
    pltpu.make_async_copy(view, view, sem).wait()


def _column(rows):
    r = rows.shape[0]
    return jnp.concatenate([rows, jnp.zeros((128 - r, 128), F32)], axis=0).T


class Ring4:
    def __init__(self, block, i, ids, plus, minus, sems, out):
        self.block, self.plus, self.minus, self.sems, self.out = block, plus, minus, sems, out
        self.i, self.ids = i, ids
        self.up, self.down, self.far = lax.rem(i + 1, 4), lax.rem(i + 3, 4), lax.rem(i + 2, 4)

    def send(self, q, owner, forward, slot):
        buf = self.plus if forward else self.minus
        pltpu.make_async_remote_copy(
            src_ref=self.block(q, owner),
            dst_ref=buf.at[slot],
            send_sem=self.sems.at[6 if forward else 7],
            recv_sem=self.sems.at[slot if forward else 3 + slot],
            device_id=self.ids(self.up if forward else self.down),
            device_id_type=MESH,
        ).start()

    def start(self):
        self.send(0, self.far, True, 0)
        self.send(1, self.far, False, 0)

    def middle(self):
        _wait(self.plus.at[0], self.sems.at[0])
        ref = self.block(0, self.up)
        ref[...] = ref[...] + self.plus[0]
        self.send(0, self.up, True, 2)
        _wait(self.minus.at[0], self.sems.at[3])
        ref = self.block(1, self.down)
        ref[...] = ref[...] + self.minus[0]
        self.send(1, self.down, False, 2)
        self.send(1, self.up, True, 1)
        self.send(0, self.down, False, 1)

    def finish(self):
        for s in (1, 2):
            _wait(self.plus.at[s], self.sems.at[s])
            _wait(self.minus.at[s], self.sems.at[3 + s])
        self.out[0] = self.block(0, self.i)[...] + (self.plus[2] + self.minus[1])
        self.out[1] = self.block(1, self.i)[...] + (self.plus[1] + self.minus[2])

    def drain(self):
        _wait(self.plus, self.sems.at[6])
        _wait(self.minus, self.sems.at[7])


class Ring8:
    def __init__(self, data, z, ids, plus, minus, sems):
        self.data, self.z, self.plus, self.minus, self.sems = data, z, plus, minus, sems
        self.next, self.last = ids(lax.rem(z + 1, 8)), ids(lax.rem(z + 7, 8))

    def send(self, step, src_up, src_down):
        lo, hi = (0, 2) if step == 0 else (4 * step - 2, 4 * step + 2)
        for src, buf, device, side in ((src_up, self.plus, self.next, 0), (src_down, self.minus, self.last, 1)):
            pltpu.make_async_remote_copy(
                src_ref=src, dst_ref=buf.at[lo:hi], send_sem=self.sems.at[8 + side],
                recv_sem=self.sems.at[4 * side + step], device_id=device, device_id_type=MESH).start()

    def start(self):
        far = lax.rem(self.z + 4, 8)
        self.send(0, self.data.at[far, 0:2], self.data.at[far, 2:4])

    def step(self, k):
        lo, hi = (0, 2) if k == 1 else (4 * k - 6, 4 * k - 2)
        up, down = lax.rem(self.z + 4 - k, 8), lax.rem(self.z + 4 + k, 8)
        for buf, at, part, side in ((self.plus, up, slice(0, 2), 0), (self.minus, down, slice(2, 4), 1)):
            _wait(buf.at[lo:hi], self.sems.at[4 * side + k - 1])
            ref = self.data.at[at, part] if k == 1 else self.data.at[at]
            ref[...] = ref[...] + buf[lo:hi]
        self.send(k, self.data.at[up], self.data.at[down])

    def finish(self, out):
        for side, buf in enumerate((self.plus, self.minus)):
            _wait(buf.at[10:14], self.sems.at[4 * side + 3])
        out[...] = self.data[self.z] + (self.plus[10:14] + self.minus[10:14])

    def drain(self):
        _wait(self.plus, self.sems.at[8])
        _wait(self.minus, self.sems.at[9])


def kernel(cells_all, counts, basis, scale, cells, cell_basis, gene_side,
           cbuf, bbuf, sbc, sk, wt, gl, gr, gp, zr, gz, gfull, w, tmp, stg, S, R, SZ, RZ, ZP, ZM, zt, zq,
           XP, XM, YP, YM, PX, PY, X2P, X2M, Y2P, Y2M, Q, zs, z3,
           high, low_part, load_sem, gsem, csem, rsem, zsem, qsem):
    sec = lax.axis_index("section")
    y = lax.axis_index("atlas")
    c = lax.rem(sec, 2)
    x = lax.rem(sec // 2, NX)
    z = sec // (2 * NX)
    h = x * NY + y

    def z_id(k):
        return ((k * NX + x) * 2 + c, y)

    def x_id(k):
        return ((z * NX + k) * 2 + c, y)

    def y_id(k):
        return (sec, k)

    partner = (sec + 1 - 2 * c, y)
    others = []
    for dx in (2, 1, 3, 0):
        for dy in (2, 1, 3, 0):
            if dx or dy:
                px, py = lax.rem(x + dx, NX), lax.rem(y + dy, NY)
                others.append((dx * NY + dy, px * NY + py, [((z * NX + px) * 2 + b, py) for b in range(2)]))

    def put(src, dst, pair, device):
        pltpu.make_async_remote_copy(
            src_ref=src, dst_ref=dst, send_sem=pair.at[0], recv_sem=pair.at[1],
            device_id=device, device_id_type=MESH).start()

    def by_core(fn):
        for b in range(2):
            pl.when(c == b)(functools.partial(fn, b))

    def alone(fn):
        pl.when(sec >= 0)(fn)

    def loads(k):
        cols = slice(CUTS[k], CUTS[k + 1])
        return (pltpu.make_async_copy(counts.at[:, cols], cbuf.at[:, cols], load_sem.at[0, k]),
                pltpu.make_async_copy(basis.at[cols, :], bbuf.at[cols, :], load_sem.at[1, k]))

    @alone
    def _():
        for k in range(CHUNKS):
            for copy in loads(k):
                copy.start()

    barrier = pltpu.get_barrier_semaphore()
    for _, _, ids in others:
        for device in ids:
            pl.semaphore_signal(barrier, inc=1, device_id=device, device_id_type=MESH)
    pl.semaphore_signal(barrier, inc=1, device_id=partner, device_id_type=MESH)

    @pl.loop(1, NZ)
    def _(d):
        pl.semaphore_signal(barrier, inc=1, device_id=z_id(lax.rem(z + d, NZ)), device_id_type=MESH)

    turned = _column(scale[...])
    for g in range(scale.shape[0]):
        sbc[128 * g:128 * g + 128, :] = jnp.broadcast_to(turned[:, g:g + 1], (128, 128))
    for k in range(CHUNKS):
        for copy in loads(k):
            copy.wait()
        rows = slice(CUTS[k], CUTS[k + 1])
        factor = sbc[rows, :]
        part = bbuf[rows, :].astype(F32)
        scaled = jnp.concatenate([part[:, :128] * factor, part[:, 128:] * factor], axis=1).astype(jnp.bfloat16)
        term = jnp.dot(cbuf[:, rows], scaled, preferred_element_type=F32)
        sk[...] = term if k == 0 else sk[...] + term

    turned = _column(cells[...])
    for r in range(cells.shape[0]):
        rows = slice(128 * r, 128 * r + 128)
        factor = jnp.broadcast_to(turned[:, r:r + 1], (128, 256))
        value = sk[rows, :] * factor
        sk[rows, :] = value
        wt[rows, :] = (value * factor).astype(jnp.bfloat16)

    gram = dot(sk[...], sk[...], ((0,), (0,))) * (1.0 / cells_all)
    gl[:, 0] = gram[:128, :128].reshape(16, 8, 128)
    gl[:, 1] = gram[128:, :128].reshape(16, 8, 128)
    gl[:, 2] = gram[128:, 128:].reshape(16, 8, 128)

    pl.semaphore_wait(barrier, PLANE - 1 + NZ - 1)

    for r, chip, ids in others:
        place = (2 * r + c) * 2
        put(gl.at[chip, 0:1], gr.at[pl.ds(place, 1)], gsem.at[0], ids[0])
        put(gl.at[chip, 1:3], gr.at[pl.ds(place, 2)], gsem.at[0], ids[1])

    def to_partner(b):
        n = 2 - b
        put(gl.at[h, 1 - b:1 - b + n], gr.at[2 * b:2 * b + n], gsem.at[0], partner)
        gr[2 * b] = gl[h, b]
        gr[2 * b + 1] = gl[h, 2 * b]

    by_core(to_partner)

    def sums(batch, begin, end):
        @pl.loop(begin, end)
        def _(j):
            cols = pl.ds(pl.multiple_of((4 * batch + j) * 640, 128), 640)
            part = lax.dot_general(cbuf[:, cols], wt[...], (((0,), (0,)), ((), ())), preferred_element_type=F32)
            factor = sbc[cols, :] * (1.0 / cells_all)
            stg[:, :128] = part[:, :128] * factor
            stg[:, 128:] = part[:, 128:] * factor
            for a in range(NX):
                for b in range(2):
                    for e in range(NY):
                        o = ((a * 2 + b) * NY + e) * 20
                        S[b, batch, 0, j, a, e] = stg[o:o + 8, :128]
                        S[b, batch, 1, j, a, e] = stg[o:o + 8, 128:]
                        S[b, batch, 2, j, a, e] = stg[o + 8:o + 16, :128]
                        S[b, batch, 3, j, a, e] = stg[o + 8:o + 16, 128:]
                        SZ[b, 4 * batch + j, a, e] = jnp.concatenate(
                            [stg[o + 16:o + 20, :128], stg[o + 16:o + 20, 128:]], axis=0)
            put(S.at[1 - c, batch, :, j], R.at[batch, :, j], csem.at[batch], partner)
            put(SZ.at[1 - c, 4 * batch + j], RZ.at[4 * batch + j], csem.at[2], partner)

    sums(0, 0, 4)
    sums(1, 0, 2)

    first, second, third, fourth = [], [], [], []
    for batch in range(2):
        first.append(Ring4(lambda q, o, n=batch: R.at[n, q, :, o], x, x_id,
                           XP.at[batch], XM.at[batch], rsem.at[batch, 0], PX.at[batch]))
        second.append(Ring4(lambda q, o, n=batch: R.at[n, 2 + q, :, :, o], y, y_id,
                            YP.at[batch], YM.at[batch], rsem.at[batch, 1], PY.at[batch]))
        third.append(Ring4(lambda q, o, n=batch: PX.at[n, q, :, o], y, y_id,
                           X2P.at[batch], X2M.at[batch], rsem.at[batch, 2], Q.at[batch, 0:2]))
        fourth.append(Ring4(lambda q, o, n=batch: PY.at[n, q, :, o], x, x_id,
                            Y2P.at[batch], Y2M.at[batch], rsem.at[batch, 3], Q.at[batch, 2:4]))

    def add_partner(batch):
        _wait(R.at[batch], csem.at[batch, 1])

        @pl.loop(0, 4)
        def _(u):
            for q in range(4):
                R[batch, q, u] = R[batch, q, u] + S[c, batch, q, u]

    def stage_one(batch):
        first[batch].start()
        second[batch].start()

    def stage_one_middle(batch):
        first[batch].middle()
        second[batch].middle()

    def stage_two(batch):
        first[batch].finish()
        third[batch].start()
        second[batch].finish()
        fourth[batch].start()

    def stage_two_middle(batch):
        third[batch].middle()
        fourth[batch].middle()

    def stage_three(batch):
        third[batch].finish()
        fourth[batch].finish()
        for j in range(NZ // 2):
            k = 4 * batch + j
            for t in range(4):
                zs[k, t] = Q[batch, t, j]
            d = lax.rem(k - z + NZ, NZ)

            @pl.when(d > 0)
            def _():
                put(zs.at[k], z3.at[d - 1], zsem, z_id(k))

    over = Ring8(RZ, z, z_id, ZP, ZM, qsem)

    def z_start():
        _wait(RZ, csem.at[2, 1])

        @pl.loop(0, NZ)
        def _(k):
            RZ[k] = RZ[k] + SZ[c, k]

        over.start()

    def z_finish():
        over.finish(zt)
        zq[0] = zt[x, y]
        for r, chip, ids in others:
            pltpu.make_async_remote_copy(
                src_ref=zt.at[chip // NY, lax.rem(chip, NY)], dst_ref=zq.at[r], send_sem=qsem.at[10], recv_sem=qsem.at[11],
                device_id=(ids[0][0] + c, ids[0][1]), device_id_type=MESH).start()

    add_partner(0)
    alone(lambda: stage_one(0))
    sums(1, 2, 4)

    by_core(lambda b: _wait(gr.at[0:31 * (b + 1)], gsem.at[0, 1]))
    gp[...] = jnp.sum(gr[...].reshape(PLANE, 2, 8, 128), axis=0)

    def over_z(b):
        @pl.loop(1, NZ)
        def _(d):
            put(gp.at[0:b + 1], zr.at[pl.ds(2 * (d - 1), b + 1)], gsem.at[1], z_id(lax.rem(z + d, NZ)))

    by_core(over_z)

    add_partner(1)
    alone(z_start)
    alone(lambda: stage_one(1))

    alone(lambda: stage_one_middle(0))
    alone(lambda: over.step(1))

    by_core(lambda b: _wait(zr.at[0:7 * (b + 1)], gsem.at[1, 1]))
    gz[...] = gp[...] + jnp.sum(zr[...].reshape(NZ - 1, 2, 8, 128), axis=0)

    def spread(b):
        n = b + 1
        gfull[h, b] = gz[0]
        if b:
            gfull[h, 2] = gz[1]
        for _, _, ids in others:
            put(gz.at[0:n], gfull.at[h, b:b + n], gsem.at[2], ids[b])

    by_core(spread)

    def split(value, at):
        top_part = value.astype(jnp.bfloat16)
        high[at, :] = top_part
        low_part[at, :] = (value - top_part.astype(F32)).astype(jnp.bfloat16)

    split(sk[...], slice(0, sk.shape[0]))
    alone(lambda: stage_one_middle(1))
    alone(lambda: over.step(2))
    alone(lambda: stage_two(0))

    def hand_over(b):
        n = b + 1
        _wait(gr.at[0:15 * n], gsem.at[2, 1])
        put(gfull.at[:, b:b + n], gfull.at[:, b:b + n], gsem.at[3], partner)

    by_core(hand_over)
    by_core(lambda b: _wait(gr.at[0:16 * (2 - b)], gsem.at[3, 1]))

    events = {
        (0, 4): lambda: stage_two(1),
        (0, 5): lambda: over.step(3),
        (0, 7): lambda: stage_two_middle(0),
        (0, 14): lambda: stage_two_middle(1),
        (1, 1): lambda: stage_three(0),
        (1, 3): z_finish,
        (1, 6): lambda: stage_three(1),
    }

    def hook(half, k):
        if (half, k) in events:
            with jax.named_scope(f"e{half}_{k}"):
                alone(events[half, k])

    inverse_factor(gfull, w, tmp, hook)

    _wait(z3, zsem.at[1])
    _wait(zq.at[1:16], qsem.at[11])
    own = zs[z] + jnp.sum(z3[...], axis=0)
    top = jnp.concatenate([own[0], own[1]], axis=1)
    mid = jnp.concatenate([own[2], own[3]], axis=1)
    rest = jnp.sum(zq[...], axis=0)
    low = jnp.concatenate([rest, pltpu.roll(rest, 4, 0)], axis=1)
    rows = sk.shape[0]
    split(jnp.concatenate([top, mid, low, jnp.zeros_like(low)], axis=0), slice(rows, rows + 32))
    factor = w[...]
    factor_high = factor.astype(jnp.bfloat16)
    factor_low = (factor - factor_high.astype(F32)).astype(jnp.bfloat16)

    def times(a, b):
        return lax.dot_general(a, b, (((1,), (1,)), ((), ())), preferred_element_type=F32)

    both = times(high[...], factor_high) + (times(high[...], factor_low) + times(low_part[...], factor_high))
    cell_basis[...] = both[:rows].astype(jnp.bfloat16)
    gene_side[...] = both[rows:rows + 20]

    def drain(b):
        _wait(gr.at[0:47 - b], gsem.at[0, 0])
        _wait(zr.at[0:7 * (b + 1)], gsem.at[1, 0])
        _wait(gr.at[0:15 * (b + 1)], gsem.at[2, 0])
        _wait(gr.at[0:16 * (b + 1)], gsem.at[3, 0])

    by_core(drain)
    for batch in range(2):
        _wait(R.at[batch], csem.at[batch, 0])
        for ring in (first[batch], second[batch], third[batch], fourth[batch]):
            ring.drain()
    _wait(z3, zsem.at[0])
    _wait(RZ, csem.at[2, 0])
    over.drain()
    _wait(zq.at[1:16], qsem.at[10])


def hand_on(a, b, a_out, b_out):
    a_out[...] = a[...]
    b_out[...] = b[...]


def local(counts, gene_scale, cell_scale, gene_basis):
    device_count = lax.axis_size("section") * lax.axis_size("atlas")
    rows, genes = counts.shape
    vm = lambda *s: pltpu.VMEM(s, F32)
    dma = pltpu.SemaphoreType.DMA
    shapes = (jax.ShapeDtypeStruct((rows, 256), jnp.bfloat16),
              jax.ShapeDtypeStruct((genes // device_count, 256), F32))
    result = pl.pallas_call(
        functools.partial(kernel, rows * device_count),
        out_shape=shapes,
        in_specs=[pl.BlockSpec(memory_space=pl.ANY)] * 2 + [pl.BlockSpec(memory_space=pltpu.VMEM)] * 2,
        out_specs=(pl.BlockSpec(memory_space=pltpu.VMEM),) * 2,
        scratch_shapes=[
            pltpu.VMEM((rows, genes), jnp.bfloat16), pltpu.VMEM((genes, 256), jnp.bfloat16),
            vm(genes, 128), vm(rows, 256), pltpu.VMEM((rows, 256), jnp.bfloat16),
            vm(16, 3, 8, 128), vm(64, 8, 128), vm(2, 8, 128), vm(14, 8, 128), vm(2, 8, 128),
            vm(16, 3, 8, 128), vm(256, 256), vm(128, 128), vm(640, 256),
            vm(2, 2, 4, 4, NX, NY, 8, 128), vm(2, 4, 4, NX, NY, 8, 128),
            vm(2, NZ, NX, NY, 8, 128), vm(NZ, NX, NY, 8, 128), vm(14, NY, 8, 128), vm(14, NY, 8, 128),
            vm(NX, NY, 8, 128), vm(NX * NY, 8, 128),
            vm(2, 3, 4, 4, 8, 128), vm(2, 3, 4, 4, 8, 128), vm(2, 3, 4, 4, 8, 128), vm(2, 3, 4, 4, 8, 128),
            vm(2, 2, 4, 4, 8, 128), vm(2, 2, 4, 4, 8, 128),
            vm(2, 3, 4, 8, 128), vm(2, 3, 4, 8, 128), vm(2, 3, 4, 8, 128), vm(2, 3, 4, 8, 128),
            vm(2, 4, 4, 8, 128), vm(NZ, 4, 8, 128), vm(NZ - 1, 4, 8, 128),
            pltpu.VMEM((rows + 32, 256), jnp.bfloat16), pltpu.VMEM((rows + 32, 256), jnp.bfloat16),
            dma((2, CHUNKS)), dma((4, 2)), dma((3, 2)), dma((2, 4, 8)), dma((2,)), dma((12,)),
        ],
        compiler_params=pltpu.CompilerParams(collective_id=0, has_side_effects=True, vmem_limit_bytes=60 << 20),
    )(counts, gene_basis, gene_scale.reshape(genes // 128, 128), cell_scale.reshape(rows // 128, 128))
    return pl.pallas_call(hand_on, out_shape=shapes)(*result)


def solution(mesh):
    return jax.shard_map(
        local,
        mesh=mesh,
        in_specs=(P(("section", "atlas"), None), P(), P(("section", "atlas")), P()),
        out_specs=(P(("section", "atlas"), None), P(("section", "atlas"), None)),
        check_vma=False,
    )
```
